128 devices in a mesh: gx: 8 (over x, core), gy: 16 (over y, z).
Axes of the slice: x: 4, y: 4, z: 4, core: 2. Of those that a mesh axis runs over, the one named last changes fastest.
Arguments:
- particles: float32 [16, 1048576], P(None, ('gx', 'gy')), may hold values from -10 to 10
- migrant_index: int32 [512, 512], P(('gx', 'gy')), may hold values from 0 to 8191, as said below
- migrant_count: int32 [128, 4], P(('gx', 'gy')), may hold values from 170 to 512, as said below
- migrated_slot_cell: int32 [1310720], P(('gx', 'gy')), may hold values from 0 to 12287
- source_tile_size: int32 [128, 256], P(('gx', 'gy')), may hold values from 1 to 64, 12288 in all within a row
- tile_owner: int32 [32768, 1], P(('gx', 'gy')), may hold values from 0 to 127; in each aligned block of 256 rows (0 to 255, 256 to 511, ...) at most 4 rows name the same one
- tile_offset: int32 [32768], P(('gx', 'gy')), may hold values from 0 to 8128, as said below
- closure: float32 [8, 16], replicated, may hold values from -1.5 to 1.5
- damping: float32 [8], replicated, may hold values from 0.5 to 1.5
Outputs:
- drag_field: bfloat16 [8, 64, 128, 128], P(None, 'gx', 'gy')
- particle_force: float32 [8, 1310720], P(None, ('gx', 'gy'))
The draws below stay inside these ranges and needn't reach their ends.
Inputs may be any that keep to these rules, and one draw needn't show every extreme that they name: `migrant_index`: on each device the first migrant_count entries of its four rows name distinct particles of that device. `migrant_count`: some device's count reaches 512. `source_tile_size`: the sizes of one device sum to 12288. `tile_owner`: among the tiles of one device no owner is named more than 4 times, a bound that some block reaches. Every tile lies in one vertical column of its owner's block: tile_offset % 128 + 64 <= 128.
All inputs are finite; a program needn't handle non-finite values.
Results may differ from the reference program's by a relative error of at most 0.0053.
Values may be sent and summed in bfloat16 or wider, within the bound.
A program may use at most 64 MiB of HBM per device.

```python
import math
import jax
import jax.numpy as jnp
import numpy as np
from jax import lax

CHANNELS = 16
DRAG_CH = 8
PART_DEV = 8192
MIGRANTS = 512
SOURCE_TILES = 256
MAX_TILE_CELLS = 64
FX = 8
FY = 8
FZ = 128
PARTICLE_CELLS = 12288
CAP = 4
TILES = 32768
PARTICLES = 1048576
MIGRATED_SLOTS = 1310720
N_GX = 8
N_GY = 16


def draw_migrant_index(key, part):
    devices = N_GX * N_GY
    keys = jax.random.split(key, devices)

    def choose(single):
        return jax.random.permutation(single, PART_DEV)[:4 * MIGRANTS]
    picked = jax.vmap(choose)(keys)
    return picked.reshape(devices * 4, MIGRANTS).astype(jnp.int32)


def draw_migrant_count(key, part):
    devices = N_GX * N_GY
    counts = jax.random.randint(key, (devices, 4), MIGRANTS // 3, MIGRANTS + 1)
    return counts.at[0, 0].set(MIGRANTS).astype(jnp.int32)


def draw_tile_offset(key, part):
    first_key = jax.random.fold_in(key, 11)
    second_key = jax.random.fold_in(key, 23)
    total_tiles = SOURCE_TILES * N_GX * N_GY
    column = jax.random.randint(first_key, (total_tiles,), 0, FX * FY)
    height = jax.random.randint(second_key, (total_tiles,), 0, FZ - MAX_TILE_CELLS + 1)
    return (column * FZ + height).astype(jnp.int32)


def place_ends(result, stream_key, smallest, largest):
    spot = [jax.random.randint(jax.random.fold_in(stream_key, axis), (), 0, length) for axis, length in enumerate(result.shape)]
    widest = result.shape.index(max(result.shape))
    next_to = spot[:widest] + [(spot[widest] + 1) % result.shape[widest]] + spot[widest + 1:]
    return result.at[tuple(spot)].set(smallest).at[tuple(next_to)].set(largest)


def levels(stream_key, extent, pieces, low, high):
    def one(position, blocks):
        heights = jax.random.uniform(jax.random.fold_in(jax.random.fold_in(stream_key, 6), position), (blocks,), jnp.float32, low / len(pieces), high / len(pieces))
        return jnp.repeat(jnp.exp(heights), extent[position] // blocks).reshape((-1,) + (1,) * (len(extent) - position - 1))

    loudness = one(*pieces[0])
    for cut in pieces[1:]:
        loudness = loudness * one(*cut)
    return loudness


def profile(count, total, reach, lean):
    loads = [(1 << 20) // math.isqrt(standing ** lean) + 1 for standing in range(2, count + 1)]
    spare, given = total - reach - (count - 1), [1] * (count - 1)
    while spare > 0:
        free = [i for i in range(count - 1) if given[i] < reach]
        mass, budget = sum([loads[i] for i in free]), spare
        for i in free:
            extra = min(reach - given[i], max(1, budget * loads[i] // mass), spare)
            given[i] = given[i] + extra
            spare = spare - extra
    return np.array([reach] + given)


def ragged_sizes(key, number_of, total, most, slope):
    if number_of == 2:
        one = jax.random.randint(key, (), max(1, total - most), min(most, total - 1) + 1)
        return jnp.stack([one, total - one])
    tallies = jnp.asarray(profile(number_of, total, most, slope), jnp.int32)
    twos = (number_of - 1) // 2
    giver, receiver = tallies[1:1 + 2 * twos:2], tallies[2:2 + 2 * twos:2]
    slack = jnp.minimum(giver - 1, most - receiver)
    moved = jax.random.randint(jax.random.fold_in(key, 1), (twos,), 0, 1 << 20) % (slack + 1)
    tallies = tallies.at[1:1 + 2 * twos:2].set(giver - moved).at[2:2 + 2 * twos:2].set(receiver + moved)
    return tallies[jax.random.permutation(jax.random.fold_in(key, 2), number_of)]


def shared_out(rng, own, number, rows, count, top, limit, slope):
    ranking = jax.random.permutation(rng, count)
    heavy_load, ordinary = load_shares(count, rows * top, limit, slope, True), load_shares(count, rows * top, limit, slope, False)
    places = jnp.arange(count)

    def named(sizes, turn):
        used = int((sizes > 0).sum())
        fixed = max(1, used // 4)
        shifted = fixed + (places - fixed + turn * (used - fixed)) % max(1, count - fixed)
        return jnp.zeros((count,), jnp.int32).at[ranking[jnp.where(places < fixed, places, shifted)]].set(jnp.asarray(sizes, jnp.int32))

    sizes = jnp.where(number % 4 == 0, named(heavy_load, number // 4), named(ordinary, number - number // 4 - 1))
    mixed = jax.random.permutation(jax.random.fold_in(own, 3), count)
    source_of, taker = mixed[0:count // 2 * 2:2], mixed[1:count // 2 * 2:2]
    room = jnp.minimum(sizes[source_of] - 1, limit - sizes[taker]) // 2
    room = jnp.where((source_of == ranking[0]) | (taker == ranking[0]) | (sizes[taker] == 0), 0, jnp.maximum(room, 0))
    shifted = jax.random.randint(jax.random.fold_in(own, 4), (count // 2,), 0, 1 << 20) % (room + 1)
    sizes = sizes.at[source_of].add(-shifted).at[taker].add(shifted)
    items = jnp.searchsorted(jnp.cumsum(sizes), jnp.arange(rows * top), side="right").astype(jnp.int32)
    listing = items.reshape(top, rows).T
    listing = listing[jax.random.permutation(jax.random.fold_in(own, 1), rows)]
    turn = jax.random.randint(jax.random.fold_in(own, 2), (rows, 1), 0, top)
    return jnp.take_along_axis(listing, (jnp.arange(top)[None, :] + turn) % top, axis=1)


def load_shares(number_of, total, limit, slope, full):
    loads = [(1 << 20) // math.isqrt(standing ** slope) + 1 for standing in range(1, number_of + 1)]
    largest = limit if full else min(limit, max(-(-total // number_of), total * loads[0] // sum(loads)))
    least = 1 if total - largest >= number_of - 1 else 0
    given, rest = [largest] + [least] * (number_of - 1), total - largest - least * (number_of - 1)
    while rest > 0:
        candidates = [i for i in range(1, number_of) if given[i] < largest] or [i for i in range(1, number_of) if given[i] < limit]
        pool, budget = sum([loads[i] for i in candidates]), rest
        for i in candidates:
            more = min(limit - given[i], max(1, budget * loads[i] // pool), rest)
            given[i] = given[i] + more
            rest = rest - more
    return np.array(given)


def noise(key, dims, spread, bound, shards=(), held_as=jnp.bfloat16):
    result = jax.random.normal(key, dims, jnp.float32) * spread
    if len(shards) > 0:
        result = levels(key, dims, shards, -0.22, 0.18) * result
    return jnp.clip(result, min=-bound, max=bound).astype(held_as)


def setup_inputs(seed: int = 0) -> dict:
    arg_keys = jax.random.split(jax.random.key(seed), 10)
    particles = noise(arg_keys[0], (CHANNELS, PARTICLES), 2.0, 10.0, ((1, 128),), jnp.float32)
    migrant_index = draw_migrant_index(jax.random.fold_in(arg_keys[9], 71), 0)
    migrant_count = draw_migrant_count(jax.random.fold_in(arg_keys[9], 71), 0)
    migrated_slot_cell = place_ends(jax.random.randint(arg_keys[3], (MIGRATED_SLOTS,), 0, PARTICLE_CELLS), jax.random.fold_in(arg_keys[3], 1), 0, PARTICLE_CELLS - 1).astype(jnp.int32)
    source_tile_size = jax.vmap(lambda own: ragged_sizes(own, SOURCE_TILES, PARTICLE_CELLS, MAX_TILE_CELLS, 1))(jax.random.split(arg_keys[4], (N_GX * N_GY))).reshape((N_GX * N_GY, SOURCE_TILES)).astype(jnp.int32)
    tile_owner_keys = jax.random.split(jax.random.fold_in(arg_keys[5], 1), TILES // SOURCE_TILES)
    tile_owner_turns = jax.random.permutation(jax.random.fold_in(arg_keys[5], 3), TILES // SOURCE_TILES)
    tile_owner = jax.vmap(lambda own, number: shared_out(jax.random.fold_in(arg_keys[5], 2), own, number, SOURCE_TILES, N_GX * N_GY, 1, CAP, 2))(tile_owner_keys, tile_owner_turns).reshape((TILES, 1))
    tile_offset = draw_tile_offset(jax.random.fold_in(arg_keys[9], 71), 0)
    closure = noise(arg_keys[7], (DRAG_CH, CHANNELS), CHANNELS ** -0.5, 1.5, (), jnp.float32)
    damping = jnp.clip(1.0 + 0.1 * jax.random.normal(arg_keys[8], (DRAG_CH,), jnp.float32), 0.5, 1.5)
    return {"particles": particles, "migrant_index": migrant_index, "migrant_count": migrant_count, "migrated_slot_cell": migrated_slot_cell, "source_tile_size": source_tile_size, "tile_owner": tile_owner, "tile_offset": tile_offset, "closure": closure, "damping": damping}


def reference(particles, migrant_index, migrant_count, migrated_slot_cell, source_tile_size, tile_owner, tile_offset, closure, damping):
    devices = N_GX * N_GY
    channel_count = particles.shape[0]
    drag_row_values = closure.shape[0]
    slots_dev = PART_DEV + 4 * MIGRANTS
    fluid_cells = FX * FY * FZ
    per_dev = particles.reshape(channel_count, devices, PART_DEV).transpose(1, 0, 2)
    lists = migrant_index.reshape(devices, 4, MIGRANTS).astype(jnp.int32)
    valid_rows = jnp.arange(MIGRANTS, dtype=jnp.int32)[None, None, :] < migrant_count[:, :, None]
    leaving = jnp.where(valid_rows, lists, PART_DEV).astype(jnp.int32)

    def clear_rows(rows):
        return jnp.ones((PART_DEV,), jnp.float32).at[rows.reshape(-1)].set(0.0, mode="drop")

    resident_live = jax.vmap(clear_rows)(leaving)
    picked = jax.vmap(lambda block, rows: block[:, rows])(per_dev, lists)
    outgoing = jnp.where(valid_rows[:, :, None, :], picked.transpose(0, 2, 1, 3), 0.0)
    sent_live = valid_rows.astype(jnp.float32)

    def arrive(cell_values):
        grid = cell_values.reshape((N_GX, N_GY) + cell_values.shape[1:])
        moved = jnp.stack([jnp.roll(grid[:, :, 0], 1, axis=0), jnp.roll(grid[:, :, 1], -1, axis=0),
                           jnp.roll(grid[:, :, 2], 1, axis=1), jnp.roll(grid[:, :, 3], -1, axis=1)], axis=2)
        return moved.reshape((devices,) + cell_values.shape[1:])

    arrived_state = arrive(outgoing).transpose(0, 2, 1, 3).reshape(devices, channel_count, 4 * MIGRANTS)
    arrived_live = arrive(sent_live).reshape(devices, 4 * MIGRANTS)
    slot_state = jnp.concatenate([per_dev, arrived_state], axis=2)
    slot_live = jnp.concatenate([resident_live, arrived_live], axis=1)
    deposit = (slot_state * slot_live[:, None, :]).astype(jnp.bfloat16)
    cell_rows = migrated_slot_cell.reshape(devices, slots_dev)

    def deposit_one(cell_values, cell_index_list):
        return jax.ops.segment_sum(cell_values.T.astype(jnp.float32), cell_index_list, num_segments=PARTICLE_CELLS)

    source_field = jax.vmap(deposit_one)(deposit, cell_rows)
    sizes = source_tile_size.astype(jnp.int32)
    tile_starts = jnp.cumsum(sizes, axis=1).astype(jnp.int32) - sizes

    def tile_ids(tile_sizes_row):
        return jnp.repeat(jnp.arange(SOURCE_TILES, dtype=jnp.int32), tile_sizes_row, total_repeat_length=PARTICLE_CELLS)

    cell_tile_index = jax.vmap(tile_ids)(sizes).astype(jnp.int32)
    within_tile_mask = jnp.arange(PARTICLE_CELLS, dtype=jnp.int32)[None, :] - jnp.take_along_axis(tile_starts, cell_tile_index, axis=1)
    owners = tile_owner.reshape(devices, SOURCE_TILES).astype(jnp.int32)
    offsets = tile_offset.reshape(devices, SOURCE_TILES).astype(jnp.int32)
    target_cells = (jnp.take_along_axis(owners, cell_tile_index, axis=1) * fluid_cells
              + jnp.take_along_axis(offsets, cell_tile_index, axis=1) + within_tile_mask).astype(jnp.int32)
    gas_flat = jnp.zeros((devices * fluid_cells, channel_count), jnp.float32).at[target_cells.reshape(-1)].add(
        source_field.reshape(-1, channel_count))
    gas_source = gas_flat.reshape(N_GX, N_GY, FX, FY, FZ, channel_count).transpose(5, 0, 2, 1, 3, 4).reshape(
        channel_count, N_GX * FX, N_GY * FY, FZ)
    weights = (1.0, 2.0, 1.0)
    smoothed = jnp.zeros_like(gas_source)
    for first in range(3):
        for second in range(3):
            moved = jnp.roll(jnp.roll(gas_source, 1 - first, axis=1), 1 - second, axis=2)
            smoothed = smoothed + (weights[first] * weights[second] / 16.0) * moved
    mixed = jnp.einsum("rf,fxyz->rxyz", closure, smoothed, precision=lax.Precision.HIGHEST)
    drag_field = (mixed / (1.0 + smoothed[0] * smoothed[0])).astype(jnp.bfloat16)
    flattened_drag = drag_field.reshape(drag_row_values, N_GX, FX, N_GY, FY, FZ).transpose(1, 3, 2, 4, 5, 0).reshape(
        devices * fluid_cells, drag_row_values)
    particle_drag = flattened_drag[target_cells]
    looked_values = jax.vmap(lambda lookup_table, cell_index_list: lookup_table[cell_index_list])(particle_drag, cell_rows).astype(jnp.float32)
    slip = slot_state[:, :drag_row_values, :].transpose(0, 2, 1)
    force = slot_live[:, :, None] * (looked_values - damping[None, None, :] * slip)
    particle_force = force.transpose(2, 0, 1).reshape(drag_row_values, devices * slots_dev)
    return drag_field, particle_force
```

```python
import jax
import jax.numpy as jnp
from jax import lax
from jax.experimental import pallas as pl
from jax.experimental.pallas import tpu as pltpu
from jax.sharding import PartitionSpec as P

F32 = jnp.float32
BF16 = jnp.bfloat16
I32 = jnp.int32
MESH = pl.DeviceIdType.MESH

N_GX = 8
N_GY = 16
N = N_GX * N_GY
CH = 16
DR = 8
PART = 8192
MIG = 512
SLOTS = PART + 4 * MIG
TILES = 256
FX = 8
FY = 8
FZ = 128
W = 256
BLOCKS = SLOTS // W
RES = PART // W
PER = 4
CHUNKS = BLOCKS // PER
KC = PER * W
ND = 32
NB = N // ND
SB = 16
NSB = N // SB
HIGH = 32
SIDES = tuple((dx, dy) for dx in (-1, 0, 1) for dy in (-1, 0, 1) if dx or dy)


def dot_nn(a, b):
    return lax.dot_general(a, b, (((1,), (0,)), ((), ())), preferred_element_type=F32)


def dot_nt(a, b):
    return lax.dot_general(a, b, (((1,), (1,)), ((), ())), preferred_element_type=F32)


def iota(shape, dim):
    return lax.broadcasted_iota(I32, shape, dim)


def wait_bytes(ref, sem):
    pltpu.make_async_copy(ref, ref, sem).wait()


def body(
    part, midx, cnt, cell, size, owner, toff, clos, damp,
    drag_o, force_o,
    pt, smig, rmig, live, rel_a, rel_b, lall, m16s, den16s, abuf, acc,
    sendm, sendd, recvm, recvd, lg, low_s, high_s, gas, dtmp, tab, sendr, retm, rbuf,
    mig_ss, mig_rs, am_ss, am_rs, ad_ss, ad_rs, halo_ss, halo_rs, back_ss, back_rs,
):
    gx = lax.axis_index("gx")
    gy = lax.axis_index("gy")
    me = gx * N_GY + gy

    def ahead(rel):
        target = lax.rem(me + rel, N)
        return (lax.div(target, N_GY), lax.rem(target, N_GY))

    def beside(dx, dy):
        return (lax.rem(gx + dx + N_GX, N_GX), lax.rem(gy + dy + N_GY, N_GY))

    barrier = pltpu.get_barrier_semaphore()

    @pl.loop(1, N)
    def _(rel):
        pl.semaphore_signal(barrier, 1, device_id=ahead(rel), device_id_type=MESH)

    @pl.loop(0, RES)
    def _(g):
        lanes = pl.ds(pl.multiple_of(g * W, W), W)
        pt[pl.ds(pl.multiple_of(g * CH, CH), CH), :] = part[:, lanes].astype(BF16)

    hits = jnp.zeros((RES, W), F32)
    for j in range(4):
        entry = midx[j : j + 1, :]
        low = entry & (W - 1)
        high = entry >> 8
        valid = iota((1, MIG), 1) < cnt[0, j]
        low_hot = jnp.where(iota((W, MIG), 0) == low, 1.0, 0.0).astype(BF16)
        picked = dot_nn(pt[...], low_hot)
        state = jnp.zeros((CH, MIG), F32)
        high_b = jnp.broadcast_to(high, (CH, MIG))
        for g in range(RES):
            state = jnp.where(high_b == g, picked[g * CH : (g + 1) * CH], state)
        flag = jnp.where(valid, 1.0, 0.0)
        smig[j, 0:CH] = (state * flag).astype(BF16)
        smig[j, CH : 2 * CH] = jnp.broadcast_to(flag, (CH, MIG)).astype(BF16)
        high_hot = jnp.where(iota((RES, MIG), 0) == high, flag, 0.0).astype(BF16)
        hits = hits + dot_nt(high_hot, low_hot)
    live[0:RES] = 1.0 - hits

    pl.semaphore_wait(barrier, N - 1)
    mig = []
    for j, (dx, dy) in enumerate(((1, 0), (-1, 0), (0, 1), (0, -1))):
        copy = pltpu.make_async_remote_copy(
            smig.at[j], rmig.at[j], mig_ss.at[j], mig_rs.at[j],
            device_id=beside(dx, dy), device_id_type=MESH,
        )
        copy.start()
        mig.append(copy)

    sub = iota((TILES, TILES), 0)
    lane = iota((TILES, TILES), 1)
    size_row = size[...].astype(F32)
    own_row = owner[...].astype(F32)
    start_col = jnp.sum(jnp.where(lane < sub, size_row, 0.0), axis=1, keepdims=True)
    size_col = jnp.sum(jnp.where(lane == sub, size_row, 0.0), axis=1, keepdims=True)
    start_row = jnp.sum(jnp.where(sub < lane, size_col, 0.0), axis=0, keepdims=True)
    own_col = jnp.sum(jnp.where(lane == sub, own_row, 0.0), axis=1, keepdims=True)
    earlier = jnp.where(own_col == own_row, jnp.where(sub < lane, 1.0, 0.0), 0.0)
    rank_row = jnp.sum(earlier, axis=0, keepdims=True)
    rel_row = own_row - me.astype(F32)
    rel_row = jnp.where(rel_row < 0.0, rel_row + N, rel_row)
    base_row = 64.0 * rank_row - start_row
    sub8 = iota((8, TILES), 0)
    values = jnp.where(sub8 == 0, rel_row, jnp.where(sub8 == 1, base_row, 0.0))
    before = jnp.where(iota((8, TILES), 1) == 0, 0.0, pltpu.roll(values, 1, 1))
    steps = (values - before).astype(BF16)

    offs = toff[...]
    xx = offs >> 10
    off_low = ((xx & 1) * FZ + (offs & (FZ - 1))).astype(F32)
    off_high = ((xx >> 1) * FY + ((offs >> 7) & (FY - 1))).astype(F32)
    sub128 = iota((N, TILES), 0)
    rank_of = (sub128 & 3).astype(F32)
    what = jnp.where(sub128 < 4, off_low, jnp.where(sub128 < 8, off_high, 0.0))
    what = jnp.where(rank_row == rank_of, what, 0.0).astype(BF16)
    rel_hot = jnp.where(sub128.astype(F32) == rel_row, 1.0, 0.0).astype(BF16)
    meta = dot_nt(rel_hot, what)
    for d in range(N):
        sendd[d, :, W : W + 128] = meta[d : d + 1, :]

    clos_f = clos[...]
    clos_hi = clos_f.astype(BF16)
    clos_lo = (clos_f - clos_hi.astype(F32)).astype(BF16)
    clos2 = jnp.concatenate([clos_hi.astype(F32), clos_lo.astype(F32)], axis=0).astype(BF16)

    sub16 = iota((16, W), 0)

    def prepare(g, dep):
        row = jnp.concatenate([cell[pl.ds(2 * g, 1), :], cell[pl.ds(2 * g + 1, 1), :]], axis=1)
        row = row.astype(F32)
        inside = jnp.where(start_col <= row, 1.0, 0.0).astype(BF16)
        found = dot_nn(steps, inside)
        rel = found[0:1]
        place = row + found[1:2]
        hot = jnp.where(iota((W, W), 0).astype(F32) == place, 1.0, 0.0).astype(BF16)
        lall[lax.div(g, PER), :, pl.ds(pl.multiple_of(lax.rem(g, PER) * W, W), W)] = hot
        rel_a[g] = (rel - jnp.where(sub16 >= 8, 1.0, 0.0)).astype(BF16)
        rel_b[g] = (rel - sub16.astype(F32)).astype(BF16)
        mixed = dot_nn(clos2, dep)
        mixed = mixed[0:8] + mixed[8:16]
        m16s[g] = jnp.concatenate([mixed, mixed], axis=0).astype(BF16)
        den16s[g] = jnp.broadcast_to(dep[0:1].astype(F32), (16, W)).astype(BF16)

    @pl.loop(0, RES)
    def _(g):
        lanes = pl.ds(pl.multiple_of(g * W, W), W)
        prepare(g, (part[:, lanes] * live[pl.ds(g, 1), :]).astype(BF16))

    for copy in mig:
        copy.wait_recv()
    for j in range(4):
        for h in range(2):
            g = RES + 2 * j + h
            live[g : g + 1] = rmig[j, CH : 2 * CH, h * W : (h + 1) * W].astype(F32)[0:1]
            prepare(g, rmig[j, 0:CH, h * W : (h + 1) * W])

    zero16 = jnp.zeros((16, W), BF16)
    for block in range(NB):
        @pl.loop(0, CHUNKS)
        def _(c):
            for i in range(PER):
                g = c * PER + i
                at = slice(i * W, (i + 1) * W)
                near, m16 = rel_a[g], m16s[g]
                for k in range(ND // 2):
                    abuf[k * 16 : (k + 1) * 16, at] = jnp.where(
                        near == float(block * ND + 2 * k), m16, zero16
                    )
                near, den = rel_b[g], den16s[g]
                for k in range(ND // 16):
                    abuf[ND * 8 + k * 16 : ND * 8 + (k + 1) * 16, at] = jnp.where(
                        near == float(block * ND + 16 * k), den, zero16
                    )
            part_sum = dot_nt(abuf[0 : ND * 9], lall[c])

            @pl.when(c == 0)
            def _():
                acc[0 : ND * 9] = part_sum

            @pl.when(c > 0)
            def _():
                acc[0 : ND * 9] += part_sum

        sendm[block * ND : (block + 1) * ND] = (
            acc[0 : ND * 8].reshape(ND, 8, W).astype(BF16)
        )
        den = acc[ND * 8 : ND * 9]
        for d in range(ND):
            sendd[block * ND + d, :, 0:W] = den[d : d + 1]
        if block == 0:
            recvm[0] = sendm[0]
            recvd[0] = sendd[0]

        @pl.loop(1 if block == 0 else block * ND, (block + 1) * ND)
        def _(rel):
            sb = lax.div(rel, SB)
            target = ahead(rel)
            pltpu.make_async_remote_copy(
                sendm.at[rel], recvm.at[rel], am_ss.at[sb], am_rs.at[sb],
                device_id=target, device_id_type=MESH,
            ).start()
            pltpu.make_async_remote_copy(
                sendd.at[rel], recvd.at[rel], ad_ss.at[sb], ad_rs.at[sb],
                device_id=target, device_id_type=MESH,
            ).start()

    def span(b):
        return pl.ds(1, SB - 1) if b == 0 else pl.ds(b * SB, SB)

    lane_row = iota((1, W), 1)
    inner = (lane_row & 63).astype(F32)
    which = lane_row >> 6
    for b in range(NSB):
        wait_bytes(recvm.at[span(b)], am_rs.at[b])
        wait_bytes(recvd.at[span(b)], ad_rs.at[b])

        @pl.loop(0, SB // PER)
        def _(q):
            for i in range(PER):
                s = b * SB + q * PER + i
                at = slice(i * W, (i + 1) * W)
                small = recvd[s]
                low = jnp.zeros((1, W), F32)
                high = jnp.zeros((1, W), F32)
                for j in range(4):
                    low = jnp.where(which == j, small[:, W + j : W + j + 1], low)
                    high = jnp.where(which == j, small[:, W + 4 + j : W + 5 + j], high)
                low = low + inner
                high_s[s] = high
                hot = jnp.where(iota((W, W), 0).astype(F32) == low, 1.0, 0.0).astype(BF16)
                lg[b * (SB // PER) + q, :, at] = hot
                mixed = recvm[s].astype(F32)
                m16 = jnp.concatenate([mixed, mixed], axis=0).astype(BF16)
                near = (high - jnp.where(sub16 >= 8, 1.0, 0.0)).astype(BF16)
                for k in range(HIGH // 2):
                    abuf[k * 16 : (k + 1) * 16, at] = jnp.where(near == float(2 * k), m16, zero16)
                den = jnp.broadcast_to(small[:, 0:W], (16, W)).astype(BF16)
                near = (high - sub16.astype(F32)).astype(BF16)
                for k in range(HIGH // 16):
                    abuf[HIGH * 8 + k * 16 : HIGH * 8 + (k + 1) * 16, at] = jnp.where(
                        near == float(16 * k), den, zero16
                    )
            part_sum = dot_nt(abuf[0 : HIGH * 9], lg[b * (SB // PER) + q])
            if b == 0:
                @pl.when(q == 0)
                def _():
                    acc[0 : HIGH * 9] = part_sum

                @pl.when(q > 0)
                def _():
                    acc[0 : HIGH * 9] += part_sum
            else:
                acc[0 : HIGH * 9] += part_sum

    for h in range(HIGH):
        for odd in range(2):
            x, y = 2 * (h // FY) + odd + 1, h % FY + 1
            at = slice(odd * FZ, (odd + 1) * FZ)
            gas[x, y, 0:8] = acc[h * 8 : (h + 1) * 8, at]
            gas[x, y, 8:16] = jnp.broadcast_to(acc[HIGH * 8 + h : HIGH * 8 + h + 1, at], (8, FZ))

    def edge(step, far):
        if step == 0:
            return pl.ds(1, 8)
        if far:
            return pl.ds(0 if step > 0 else 9, 1)
        return pl.ds(8 if step > 0 else 1, 1)

    halo = []
    for i, (dx, dy) in enumerate(SIDES):
        copy = pltpu.make_async_remote_copy(
            gas.at[edge(dx, False), edge(dy, False)], gas.at[edge(dx, True), edge(dy, True)],
            halo_ss.at[i], halo_rs.at[i], device_id=beside(dx, dy), device_id_type=MESH,
        )
        copy.start()
        halo.append(copy)
    for copy in halo:
        copy.wait_recv()

    @pl.loop(0, FX // 2)
    def _(x2):
        for odd in range(2):
            x = 2 * x2 + odd
            over_x = [gas[x, y] + 2.0 * gas[x + 1, y] + gas[x + 2, y] for y in range(FY + 2)]
            got = []
            for y in range(FY):
                smooth = (over_x[y] + 2.0 * over_x[y + 1] + over_x[y + 2]) * (1.0 / 16.0)
                dens = smooth[8:16]
                drag = smooth[0:8] / (1.0 + dens * dens)
                dtmp[x, y * 8 : (y + 1) * 8] = drag
                got.append(drag)
            for y in range(0, FY, 2):
                tab[pl.ds(pl.multiple_of(x2 * 64 + y * 8, 16), 16), odd * FZ : (odd + 1) * FZ] = (
                    jnp.concatenate([got[y], got[y + 1]], axis=0).astype(BF16)
                )

    for b in range(NSB):
        @pl.loop(0, SB // PER)
        def _(q):
            for i in range(PER):
                s = b * SB + q * PER + i
                at = slice(i * W, (i + 1) * W)
                full = dot_nn(tab[...], lg[b * (SB // PER) + q, :, at])
                high = jnp.broadcast_to(high_s[s], (8, W))
                got = jnp.zeros((8, W), F32)
                for h in range(HIGH):
                    got = jnp.where(high == float(h), full[h * 8 : (h + 1) * 8], got)
                sendr[s] = got.astype(BF16)

        if b == 0:
            retm[0] = sendr[0]

        @pl.loop(1 if b == 0 else b * SB, (b + 1) * SB)
        def _(rel):
            pltpu.make_async_remote_copy(
                sendr.at[rel], retm.at[rel], back_ss.at[b], back_rs.at[b],
                device_id=ahead(N - rel), device_id_type=MESH,
            ).start()

    for r in range(DR):
        for x in range(FX):
            drag_o[r, x] = dtmp[x, pl.ds(r, FY, stride=8), :].astype(BF16)

    for b in range(NSB):
        wait_bytes(retm.at[span(b)], back_rs.at[b])
        back = retm[b * SB : (b + 1) * SB].astype(F32).reshape(SB * 8, W)
        rbuf[b * SB * 8 : (b + 1) * SB * 8] = back.astype(BF16)

    rows8 = iota((8, W), 0)
    slip = jnp.zeros((8, W), F32)
    for r in range(DR):
        slip = jnp.where(rows8 == r, damp[r], slip)

    def finish(g, c, i, state):
        hot = lall[c, :, i * W : (i + 1) * W]
        rel = jnp.broadcast_to(rel_a[g].astype(F32)[0:1], (8, W))
        got = jnp.zeros((8, W), F32)
        for b in range(NSB):
            full = dot_nn(rbuf[b * SB * 8 : (b + 1) * SB * 8], hot)
            for d in range(SB):
                got = jnp.where(rel == float(b * SB + d), full[d * 8 : (d + 1) * 8], got)
        force_o[:, pl.ds(pl.multiple_of(g * W, W), W)] = live[pl.ds(g, 1), :] * (
            got - slip * state
        )

    @pl.loop(0, RES // PER)
    def _(c):
        for i in range(PER):
            g = c * PER + i
            finish(g, c, i, part[0:8, pl.ds(pl.multiple_of(g * W, W), W)])

    for j in range(4):
        for h in range(2):
            g = RES + 2 * j + h
            finish(g, g // PER, g % PER, rmig[j, 0:CH, h * W : (h + 1) * W].astype(F32)[0:8])

    for copy in mig + halo:
        copy.wait_send()
    for b in range(NSB):
        wait_bytes(sendm.at[span(b)], am_ss.at[b])
        wait_bytes(sendd.at[span(b)], ad_ss.at[b])
        wait_bytes(sendr.at[span(b)], back_ss.at[b])


def per_device(
    particles, migrant_index, migrant_count, migrated_slot_cell, source_tile_size,
    tile_owner, tile_offset, closure, damping,
):
    vmem = pl.BlockSpec(memory_space=pltpu.VMEM)
    smem = pl.BlockSpec(memory_space=pltpu.SMEM)
    dma = pltpu.SemaphoreType.DMA
    scratch = [
        pltpu.VMEM((RES * CH, W), BF16),
        pltpu.VMEM((4, 2 * CH, MIG), BF16),
        pltpu.VMEM((4, 2 * CH, MIG), BF16),
        pltpu.VMEM((BLOCKS, W), F32),
        pltpu.VMEM((BLOCKS, 16, W), BF16),
        pltpu.VMEM((BLOCKS, 16, W), BF16),
        pltpu.VMEM((CHUNKS, W, KC), BF16),
        pltpu.VMEM((BLOCKS, 16, W), BF16),
        pltpu.VMEM((BLOCKS, 16, W), BF16),
        pltpu.VMEM((max(ND, HIGH) * 9, KC), BF16),
        pltpu.VMEM((max(ND, HIGH) * 9, W), F32),
        pltpu.VMEM((N, 8, W), BF16),
        pltpu.VMEM((N, 1, W + 128), F32),
        pltpu.VMEM((N, 8, W), BF16),
        pltpu.VMEM((N, 1, W + 128), F32),
        pltpu.VMEM((N // PER, W, KC), BF16),
        pltpu.VMEM((8, 128), F32),
        pltpu.VMEM((N, 1, W), F32),
        pltpu.VMEM((FX + 2, FY + 2, 16, FZ), F32),
        pltpu.VMEM((FX, FY * 8, FZ), F32),
        pltpu.VMEM((HIGH * 8, W), BF16),
        pltpu.VMEM((N, 8, W), BF16),
        pltpu.VMEM((N, 8, W), BF16),
        pltpu.VMEM((N * 8, W), BF16),
        dma((4,)), dma((4,)), dma((NSB,)), dma((NSB,)), dma((NSB,)), dma((NSB,)),
        dma((8,)), dma((8,)), dma((NSB,)), dma((NSB,)),
    ]
    return pl.pallas_call(
        body,
        out_shape=(
            jax.ShapeDtypeStruct((DR, FX, FY, FZ), BF16),
            jax.ShapeDtypeStruct((DR, SLOTS), F32),
        ),
        in_specs=[vmem, vmem, smem, vmem, vmem, vmem, vmem, vmem, smem],
        out_specs=(vmem, vmem),
        scratch_shapes=scratch,
        compiler_params=pltpu.CompilerParams(
            collective_id=0, has_side_effects=True, vmem_limit_bytes=60 * 1024 * 1024
        ),
    )(
        particles,
        migrant_index,
        migrant_count,
        migrated_slot_cell.reshape(2 * BLOCKS, 128),
        source_tile_size,
        tile_owner.reshape(1, TILES),
        tile_offset.reshape(1, TILES),
        closure,
        damping,
    )


def solution(mesh):
    in_specs = (
        P(None, ("gx", "gy")),
        P(("gx", "gy"), None),
        P(("gx", "gy"), None),
        P(("gx", "gy")),
        P(("gx", "gy"), None),
        P(("gx", "gy"), None),
        P(("gx", "gy")),
        P(),
        P(),
    )
    out_specs = (P(None, "gx", "gy", None), P(None, ("gx", "gy")))
    return jax.shard_map(
        per_device, mesh=mesh, in_specs=in_specs, out_specs=out_specs, check_vma=False
    )
```

```python
import jax
import jax.numpy as jnp
from jax import lax
from jax.experimental import pallas as pl
from jax.experimental.pallas import tpu as pltpu
from jax.sharding import PartitionSpec as P

F32 = jnp.float32
BF16 = jnp.bfloat16
I32 = jnp.int32
MESH = pl.DeviceIdType.MESH

N_GX = 8
N_GY = 16
N = N_GX * N_GY
CH = 16
DR = 8
PART = 8192
MIG = 512
SLOTS = PART + 4 * MIG
TILES = 256
FX = 8
FY = 8
FZ = 128
W = 256
BLOCKS = SLOTS // W
RES = PART // W
RCH = 8
LATE = 0
PER = 4
CHUNKS = BLOCKS // PER
KC = PER * W
ND = 32
NB = N // ND
SB = 16
NSB = N // SB
UN = 4
HOP = 37
BACK = 45
EXT = 128
SIDES = tuple((dx, dy) for dx in (-1, 0, 1) for dy in (-1, 0, 1) if dx or dy)


def dot_nn(a, b):
    return lax.dot_general(a, b, (((1,), (0,)), ((), ())), preferred_element_type=F32)


def dot_nt(a, b):
    return lax.dot_general(a, b, (((1,), (1,)), ((), ())), preferred_element_type=F32)


def iota(shape, dim):
    return lax.broadcasted_iota(I32, shape, dim)


def tiles2(tiles, r):
    return tiles.reshape(4 * N * 8, FZ)[pl.ds(r, 4 * N, stride=8), :].astype(BF16)


def wait_bytes(ref, sem):
    pltpu.make_async_copy(ref, ref, sem).wait()


def body(
    part, midx, cnt, cell, size, owner, toff, clos, damp,
    drag_o, force_o,
    pt, smig, rmig, live, rel_a, rel_b, lall, m16s, den16s, abuf, acc,
    sendm, ext, recvm, meta_v, meta_s, tiles, tden, flat, picked, gas, dtmp, sendr, retm, rbuf,
    mig_ss, mig_rs, am_ss, am_rs, halo_ss, halo_rs, back_ss, back_rs, meta_sem,
):
    gx = lax.axis_index("gx")
    gy = lax.axis_index("gy")
    me = gx * N_GY + gy

    def ahead(rel):
        target = (me + rel * HOP) & (N - 1)
        return (target >> 4, target & (N_GY - 1))

    def beside(dx, dy):
        return ((gx + dx) & (N_GX - 1), (gy + dy) & (N_GY - 1))

    barrier = pltpu.get_barrier_semaphore()

    @pl.loop(1, N)
    def _(rel):
        pl.semaphore_signal(barrier, 1, device_id=ahead(rel), device_id_type=MESH)

    @pl.loop(0, RES)
    def _(g):
        lanes = pl.ds(pl.multiple_of(g * W, W), W)
        pt[pl.ds(pl.multiple_of(g * CH, CH), CH), :] = part[:, lanes].astype(BF16)

    hits = jnp.zeros((RES, W), F32)
    for j in range(4):
        entry = midx[j : j + 1, :]
        low = entry & (W - 1)
        high = entry >> 8
        valid = iota((1, MIG), 1) < cnt[0, j]
        low_hot = jnp.where(iota((W, MIG), 0) == low, 1.0, 0.0).astype(BF16)
        found = dot_nn(pt[...], low_hot)
        state = jnp.zeros((CH, MIG), F32)
        high_b = jnp.broadcast_to(high, (CH, MIG))
        for g in range(RES):
            state = jnp.where(high_b == g, found[g * CH : (g + 1) * CH], state)
        flag = jnp.where(valid, 1.0, 0.0)
        smig[j, 0:CH] = (state * flag).astype(BF16)
        smig[j, CH : 2 * CH] = jnp.broadcast_to(flag, (CH, MIG)).astype(BF16)
        high_hot = jnp.where(iota((RES, MIG), 0) == high, flag, 0.0).astype(BF16)
        hits = hits + dot_nt(high_hot, low_hot)
    live[0:RES] = 1.0 - hits

    pl.semaphore_wait(barrier, N - 1)
    mig = []
    for j, (dx, dy) in enumerate(((1, 0), (-1, 0), (0, 1), (0, -1))):
        copy = pltpu.make_async_remote_copy(
            smig.at[j], rmig.at[j], mig_ss.at[j], mig_rs.at[j],
            device_id=beside(dx, dy), device_id_type=MESH,
        )
        copy.start()
        mig.append(copy)

    sub = iota((TILES, TILES), 0)
    lane = iota((TILES, TILES), 1)
    size_row = size[...].astype(F32)
    own_row = owner[...].astype(F32)
    start_col = jnp.sum(jnp.where(lane < sub, size_row, 0.0), axis=1, keepdims=True)
    size_col = jnp.sum(jnp.where(lane == sub, size_row, 0.0), axis=1, keepdims=True)
    start_row = jnp.sum(jnp.where(sub < lane, size_col, 0.0), axis=0, keepdims=True)
    own_col = jnp.sum(jnp.where(lane == sub, own_row, 0.0), axis=1, keepdims=True)
    earlier = jnp.where(own_col == own_row, jnp.where(sub < lane, 1.0, 0.0), 0.0)
    rank_row = jnp.sum(earlier, axis=0, keepdims=True)
    rel_row = (((owner[...] - me) * BACK) & (N - 1)).astype(F32)
    base_row = 64.0 * rank_row - start_row
    sub8 = iota((8, TILES), 0)
    values = jnp.where(sub8 == 0, rel_row, jnp.where(sub8 == 1, base_row, 0.0))
    before = jnp.where(iota((8, TILES), 1) == 0, 0.0, pltpu.roll(values, 1, 1))
    steps = (values - before).astype(BF16)

    offs = toff[...]
    off_low = (offs & (FZ - 1)).astype(F32)
    off_high = (offs >> 7).astype(F32)
    sub128 = iota((N, TILES), 0)
    rank_of = (sub128 & 3).astype(F32)
    what = jnp.where(sub128 < 4, off_low, jnp.where(sub128 < 8, off_high, 0.0))
    what = jnp.where(rank_row == rank_of, what, 0.0).astype(BF16)
    rel_hot = jnp.where(sub128.astype(F32) == rel_row, 1.0, 0.0).astype(BF16)
    meta = dot_nt(rel_hot, what)
    for d in range(0, N, 8):
        ext[pl.ds(d * 8 + 4, 8, stride=8), :] = meta[d : d + 8]

    clos_f = clos[...]
    clos_hi = clos_f.astype(BF16)
    clos_lo = (clos_f - clos_hi.astype(F32)).astype(BF16)
    clos2 = jnp.concatenate([clos_hi.astype(F32), clos_lo.astype(F32)], axis=0).astype(BF16)

    sub16 = iota((16, W), 0)

    def prepare(g, dep):
        row = jnp.concatenate([cell[pl.ds(2 * g, 1), :], cell[pl.ds(2 * g + 1, 1), :]], axis=1)
        row = row.astype(F32)
        inside = jnp.where(start_col <= row, 1.0, 0.0).astype(BF16)
        found = dot_nn(steps, inside)
        rel = found[0:1]
        place = row + found[1:2]
        hot = jnp.where(iota((W, W), 0).astype(F32) == place, 1.0, 0.0).astype(BF16)
        lall[lax.div(g, PER), :, pl.ds(pl.multiple_of(lax.rem(g, PER) * W, W), W)] = hot
        rel_a[g] = (rel - jnp.where(sub16 >= 8, 1.0, 0.0)).astype(BF16)
        rel_b[g] = (rel - sub16.astype(F32)).astype(BF16)
        mixed = dot_nn(clos2, dep)
        mixed = mixed[0:8] + mixed[8:16]
        m16s[g] = jnp.concatenate([mixed, mixed], axis=0).astype(BF16)
        den16s[g] = jnp.broadcast_to(dep[0:1].astype(F32), (16, W)).astype(BF16)

    @pl.loop(0, RES)
    def _(g):
        lanes = pl.ds(pl.multiple_of(g * W, W), W)
        prepare(g, (part[:, lanes] * live[pl.ds(g, 1), :]).astype(BF16))

    zero16 = jnp.zeros((16, W), BF16)

    def spread(c, first, count, row0):
        for i in range(PER):
            g = c * PER + i
            at = slice(i * W, (i + 1) * W)
            near, m16 = rel_a[g], m16s[g]
            for k in range(count // 2):
                abuf[row0 + k * 16 : row0 + (k + 1) * 16, at] = jnp.where(
                    near == float(first + 2 * k), m16, zero16
                )
            near, den = rel_b[g], den16s[g]
            for k in range(count // 16):
                abuf[row0 + count * 8 + k * 16 : row0 + count * 8 + (k + 1) * 16, at] = jnp.where(
                    near == float(first + 16 * k), den, zero16
                )

    def resident(c):
        spread(c, 0, N, 0)
        return dot_nt(abuf[...], lall[c])

    acc[...] = jnp.zeros(acc.shape, F32)

    @pl.loop(0, RCH - LATE)
    def _(c):
        acc[...] += resident(c)

    for copy in mig:
        copy.wait_recv()
    for j in range(4):
        for h in range(2):
            g = RES + 2 * j + h
            live[g : g + 1] = rmig[j, CH : 2 * CH, h * W : (h + 1) * W].astype(F32)[0:1]
            prepare(g, rmig[j, 0:CH, h * W : (h + 1) * W])

    def send_out(rel):
        sb = lax.div(rel, SB)
        pltpu.make_async_remote_copy(
            sendm.at[rel], recvm.at[rel], am_ss.at[sb], am_rs.at[sb],
            device_id=ahead(rel), device_id_type=MESH,
        ).start()

    for block in range(NB):
        rows = slice(block * ND * 8, (block + 1) * ND * 8)
        drows = slice(N * 8 + block * ND, N * 8 + (block + 1) * ND)
        mixed = acc[rows]
        den = acc[drows]
        for c in range(RCH, CHUNKS):
            base = (c - RCH) * ND * 9
            spread(c, block * ND, ND, base)
            more = dot_nt(abuf[base : base + ND * 9], lall[c])
            mixed = mixed + more[0 : ND * 8]
            den = den + more[ND * 8 : ND * 9]
        sendm[block * ND : (block + 1) * ND, :, 0:W] = mixed.reshape(ND, 8, W).astype(BF16)
        den_hi = den.astype(BF16).astype(F32)
        den_lo = den - den_hi
        for d in range(0, ND, 8):
            row = (block * ND + d) * 8
            for half in range(2):
                at = slice(half * 128, (half + 1) * 128)
                ext[pl.ds(row + half, 8, stride=8), :] = den_hi[d : d + 8, at]
                ext[pl.ds(row + 2 + half, 8, stride=8), :] = den_lo[d : d + 8, at]
        sendm[block * ND : (block + 1) * ND, :, W : W + EXT] = (
            ext[rows].reshape(ND, 8, EXT).astype(BF16)
        )
        if block == 0:
            recvm[0] = sendm[0]

        @pl.loop(1 if block == 0 else block * ND, (block + 1) * ND)
        def _(rel):
            send_out(rel)

    def span(b):
        return pl.ds(1, SB - 1) if b == 0 else pl.ds(b * SB, SB)

    lane_row = iota((1, FZ), 1)
    first_half = lane_row < 64
    for b in range(NSB):
        wait_bytes(recvm.at[span(b)], am_rs.at[b])
        ext[b * SB * 8 : (b + 1) * SB * 8] = (
            recvm[b * SB : (b + 1) * SB, :, W : W + EXT].astype(F32).reshape(SB * 8, EXT)
        )
        meta_v[b * SB : (b + 1) * SB] = ext[pl.ds(b * SB * 8 + 4, SB, stride=8), :].astype(I32)
        pltpu.make_async_copy(
            meta_v.at[pl.ds(b * SB, SB)], meta_s.at[pl.ds(b * SB, SB)], meta_sem.at[b]
        ).start()

    for b in range(NSB):
        wait_bytes(meta_s.at[pl.ds(b * SB, SB)], meta_sem.at[b])

    @pl.loop(0, N // UN)
    def _(q):
        for i in range(UN):
            s = q * UN + i
            whole = recvm[s, :, 0:W].astype(F32)
            for j in range(4):
                half = j // 2
                keep = first_half if j % 2 == 0 else ~first_half
                shift = (meta_s[s, j] + (0 if j % 2 == 0 else 64)) & (FZ - 1)
                at = slice(half * FZ, (half + 1) * FZ)
                tiles[j * N + s] = pltpu.roll(jnp.where(keep, whole[:, at], 0.0), shift, 1)
                den = ext[pl.ds(s * 8 + half, 1), :] + ext[pl.ds(s * 8 + 2 + half, 1), :]
                den = jnp.broadcast_to(jnp.where(keep, den, 0.0), (8, FZ))
                tden[pl.ds(j * N + s, 1), :] = pltpu.roll(den, shift, 1)[0:1]

    square = iota((N, N), 0) == iota((N, N), 1)
    meta_f = meta_v[...].astype(F32)
    cols = []
    for j in range(4):
        cols.append(
            jnp.sum(jnp.where(square, meta_f[:, 4 + j : 5 + j], 0.0), axis=0, keepdims=True)
        )
    col_row = jnp.concatenate(cols, axis=1)
    col_hot = jnp.where(iota((FX * FY, 4 * N), 0).astype(F32) == col_row, 1.0, 0.0)
    for r in range(0, DR, 2):
        pair = [tiles2(tiles, r), tiles2(tiles, r + 1)]
        sums = dot_nn(col_hot.astype(BF16), jnp.concatenate(pair, axis=1))
        flat[r * 64 : (r + 1) * 64] = sums[:, 0:FZ]
        flat[(r + 1) * 64 : (r + 2) * 64] = sums[:, FZ : 2 * FZ]
    den = lax.dot_general(
        col_hot, tden[...], (((1,), (0,)), ((), ())),
        precision=lax.Precision.HIGHEST, preferred_element_type=F32,
    )
    for x in range(FX):
        for y in range(FY):
            c = x * FY + y
            gas[x + 1, y + 1, 0:8] = flat[pl.ds(c, 8, stride=64), :]
            gas[x + 1, y + 1, 8:16] = jnp.broadcast_to(den[c : c + 1], (8, FZ))

    def edge(step, far):
        if step == 0:
            return pl.ds(1, 8)
        if far:
            return pl.ds(0 if step > 0 else 9, 1)
        return pl.ds(8 if step > 0 else 1, 1)

    halo = []
    for i, (dx, dy) in enumerate(SIDES):
        copy = pltpu.make_async_remote_copy(
            gas.at[edge(dx, False), edge(dy, False)], gas.at[edge(dx, True), edge(dy, True)],
            halo_ss.at[i], halo_rs.at[i], device_id=beside(dx, dy), device_id_type=MESH,
        )
        copy.start()
        halo.append(copy)
    for copy in halo:
        copy.wait_recv()

    @pl.loop(0, FX // 2)
    def _(x2):
        for odd in range(2):
            x = 2 * x2 + odd
            over_x = [gas[x, y] + 2.0 * gas[x + 1, y] + gas[x + 2, y] for y in range(FY + 2)]
            for y in range(FY):
                smooth = (over_x[y] + 2.0 * over_x[y + 1] + over_x[y + 2]) * (1.0 / 16.0)
                dens = smooth[8:16]
                drag = smooth[0:8] / (1.0 + dens * dens)
                dtmp[x, y * 8 : (y + 1) * 8] = drag

    tile_hot = jnp.concatenate(
        [
            jnp.where(iota((N, FX * FY), 1).astype(F32) == meta_f[:, 4 + j : 5 + j], 1.0, 0.0)
            for j in range(4)
        ],
        axis=0,
    ).astype(BF16)
    drag_rows = dtmp.reshape(FX * FY * 8, FZ)
    for r in range(0, DR, 2):
        pair = [drag_rows[pl.ds(r + k, FX * FY, stride=8), :].astype(BF16) for k in range(2)]
        got = dot_nn(tile_hot, jnp.concatenate(pair, axis=1))
        picked[r * 4 * N : (r + 1) * 4 * N] = got[:, 0:FZ]
        picked[(r + 1) * 4 * N : (r + 2) * 4 * N] = got[:, FZ : 2 * FZ]

    for b in range(NSB):
        @pl.loop(0, SB // UN)
        def _(q):
            for i in range(UN):
                s = b * SB + q * UN + i
                halves = []
                for half in range(2):
                    pair = []
                    for j in (2 * half, 2 * half + 1):
                        shift = ((0 if j % 2 == 0 else 64) - meta_s[s, j]) & (FZ - 1)
                        pair.append(
                            pltpu.roll(picked[pl.ds(j * N + s, 8, stride=4 * N), :], shift, 1)
                        )
                    halves.append(jnp.where(first_half, pair[0], pair[1]))
                sendr[s] = jnp.concatenate(halves, axis=1).astype(BF16)

        if b == 0:
            retm[0] = sendr[0]

        @pl.loop(1 if b == 0 else b * SB, (b + 1) * SB)
        def _(rel):
            pltpu.make_async_remote_copy(
                sendr.at[rel], retm.at[rel], back_ss.at[b], back_rs.at[b],
                device_id=ahead(N - rel), device_id_type=MESH,
            ).start()

    for r in range(DR):
        for x in range(FX):
            drag_o[r, x] = dtmp[x, pl.ds(r, FY, stride=8), :].astype(BF16)

    for b in range(NSB):
        wait_bytes(retm.at[span(b)], back_rs.at[b])
        back = retm[b * SB : (b + 1) * SB].astype(F32).reshape(SB * 8, W)
        rbuf[b * SB * 8 : (b + 1) * SB * 8] = back.astype(BF16)

    rows8 = iota((8, W), 0)
    slip = jnp.zeros((8, W), F32)
    for r in range(DR):
        slip = jnp.where(rows8 == r, damp[r], slip)

    def finish(g, c, i, state):
        hot = lall[c, :, i * W : (i + 1) * W]
        rel = jnp.broadcast_to(rel_a[g].astype(F32)[0:1], (8, W))
        got = jnp.zeros((8, W), F32)
        for b in range(NSB):
            full = dot_nn(rbuf[b * SB * 8 : (b + 1) * SB * 8], hot)
            for d in range(SB):
                got = jnp.where(rel == float(b * SB + d), full[d * 8 : (d + 1) * 8], got)
        force_o[:, pl.ds(pl.multiple_of(g * W, W), W)] = live[pl.ds(g, 1), :] * (
            got - slip * state
        )

    @pl.loop(0, RES // PER)
    def _(c):
        for i in range(PER):
            g = c * PER + i
            finish(g, c, i, part[0:8, pl.ds(pl.multiple_of(g * W, W), W)])

    for j in range(4):
        for h in range(2):
            g = RES + 2 * j + h
            finish(g, g // PER, g % PER, rmig[j, 0:CH, h * W : (h + 1) * W].astype(F32)[0:8])

    for copy in mig + halo:
        copy.wait_send()
    for b in range(NSB):
        wait_bytes(sendm.at[span(b)], am_ss.at[b])
        wait_bytes(sendr.at[span(b)], back_ss.at[b])


def per_device(
    particles, migrant_index, migrant_count, migrated_slot_cell, source_tile_size,
    tile_owner, tile_offset, closure, damping,
):
    vmem = pl.BlockSpec(memory_space=pltpu.VMEM)
    smem = pl.BlockSpec(memory_space=pltpu.SMEM)
    dma = pltpu.SemaphoreType.DMA
    scratch = [
        pltpu.VMEM((RES * CH, W), BF16),
        pltpu.VMEM((4, 2 * CH, MIG), BF16),
        pltpu.VMEM((4, 2 * CH, MIG), BF16),
        pltpu.VMEM((BLOCKS, W), F32),
        pltpu.VMEM((BLOCKS, 16, W), BF16),
        pltpu.VMEM((BLOCKS, 16, W), BF16),
        pltpu.VMEM((CHUNKS, W, KC), BF16),
        pltpu.VMEM((BLOCKS, 16, W), BF16),
        pltpu.VMEM((BLOCKS, 16, W), BF16),
        pltpu.VMEM((N * 9, KC), BF16),
        pltpu.VMEM((N * 9, W), F32),
        pltpu.VMEM((N, 8, W + EXT), BF16),
        pltpu.VMEM((N * 8, EXT), F32),
        pltpu.VMEM((N, 8, W + EXT), BF16),
        pltpu.VMEM((N, 128), I32),
        pltpu.SMEM((N, 128), I32),
        pltpu.VMEM((4 * N, 8, FZ), F32),
        pltpu.VMEM((4 * N, FZ), F32),
        pltpu.VMEM((DR * FX * FY, FZ), F32),
        pltpu.VMEM((DR * 4 * N, FZ), F32),
        pltpu.VMEM((FX + 2, FY + 2, 16, FZ), F32),
        pltpu.VMEM((FX, FY * 8, FZ), F32),
        pltpu.VMEM((N, 8, W), BF16),
        pltpu.VMEM((N, 8, W), BF16),
        pltpu.VMEM((N * 8, W), BF16),
        dma((4,)), dma((4,)), dma((NSB,)), dma((NSB,)),
        dma((8,)), dma((8,)), dma((NSB,)), dma((NSB,)), dma((NSB,)),
    ]
    return pl.pallas_call(
        body,
        out_shape=(
            jax.ShapeDtypeStruct((DR, FX, FY, FZ), BF16),
            jax.ShapeDtypeStruct((DR, SLOTS), F32),
        ),
        in_specs=[vmem, vmem, smem, vmem, vmem, vmem, vmem, vmem, smem],
        out_specs=(vmem, vmem),
        scratch_shapes=scratch,
        compiler_params=pltpu.CompilerParams(
            collective_id=0, has_side_effects=True, vmem_limit_bytes=60 * 1024 * 1024
        ),
    )(
        particles,
        migrant_index,
        migrant_count,
        migrated_slot_cell.reshape(2 * BLOCKS, 128),
        source_tile_size,
        tile_owner.reshape(1, TILES),
        tile_offset.reshape(1, TILES),
        closure,
        damping,
    )


def solution(mesh):
    in_specs = (
        P(None, ("gx", "gy")),
        P(("gx", "gy"), None),
        P(("gx", "gy"), None),
        P(("gx", "gy")),
        P(("gx", "gy"), None),
        P(("gx", "gy"), None),
        P(("gx", "gy")),
        P(),
        P(),
    )
    out_specs = (P(None, "gx", "gy", None), P(None, ("gx", "gy")))
    return jax.shard_map(
        per_device, mesh=mesh, in_specs=in_specs, out_specs=out_specs, check_vma=False
    )
```

```python
import jax
import jax.numpy as jnp
from jax import lax
from jax.experimental import pallas as pl
from jax.experimental.pallas import tpu as pltpu
from jax.sharding import PartitionSpec as P

F32 = jnp.float32
BF16 = jnp.bfloat16
I32 = jnp.int32
MESH = pl.DeviceIdType.MESH

N_GX = 8
N_GY = 16
N = N_GX * N_GY
CH = 16
DR = 8
PART = 8192
MIG = 512
SLOTS = PART + 4 * MIG
TILES = 256
FX = 8
FY = 8
FZ = 128
W = 256
BLOCKS = SLOTS // W
RES = PART // W
PER = 4
CHUNKS = BLOCKS // PER
KC = PER * W
ND = 64
NB = N // ND
SB = 16
NSB = N // SB
UN = 4
HOP = 37
BACK = 45
EXT = 128
SIDES = tuple((dx, dy) for dx in (-1, 0, 1) for dy in (-1, 0, 1) if dx or dy)


def dot_nn(a, b):
    return lax.dot_general(a, b, (((1,), (0,)), ((), ())), preferred_element_type=F32)


def dot_nt(a, b):
    return lax.dot_general(a, b, (((1,), (1,)), ((), ())), preferred_element_type=F32)


def iota(shape, dim):
    return lax.broadcasted_iota(I32, shape, dim)


def tiles2(tiles, r):
    return tiles.reshape(4 * N * 8, FZ)[pl.ds(r, 4 * N, stride=8), :].astype(BF16)


def wait_bytes(ref, sem):
    pltpu.make_async_copy(ref, ref, sem).wait()


def body(
    part, midx, cnt, cell, size, owner, toff, clos, damp,
    drag_o, force_o,
    pt, smig, rmig, live, rel_a, rel_b, lall, m16s, den16s, abuf, acc,
    sendm, ext, recvm, meta_v, meta_s, tiles, tden, flat, picked, keep8, gas, dtmp, sendr, retm, rbuf,
    mig_ss, mig_rs, am_ss, am_rs, halo_ss, halo_rs, back_ss, back_rs, meta_sem, rows_sem,
):
    gx = lax.axis_index("gx")
    gy = lax.axis_index("gy")
    me = gx * N_GY + gy

    def ahead(rel):
        target = (me + rel * HOP) & (N - 1)
        return (target >> 4, target & (N_GY - 1))

    def beside(dx, dy):
        return ((gx + dx) & (N_GX - 1), (gy + dy) & (N_GY - 1))

    barrier = pltpu.get_barrier_semaphore()

    for k in range(1, N_GY):
        pl.semaphore_signal(barrier, 1, device_id=beside(0, k), device_id_type=MESH)
    for k in range(1, N_GX):
        pl.semaphore_signal(barrier, 1, device_id=beside(k, 0), device_id_type=MESH)

    @pl.loop(0, RES)
    def _(g):
        lanes = pl.ds(pl.multiple_of(g * W, W), W)
        pt[pl.ds(pl.multiple_of(g * CH, CH), CH), :] = part[:, lanes].astype(BF16)

    hits = jnp.zeros((RES, W), F32)
    for j in range(4):
        entry = midx[j : j + 1, :]
        low = entry & (W - 1)
        high = entry >> 8
        valid = iota((1, MIG), 1) < cnt[0, j]
        low_hot = jnp.where(iota((W, MIG), 0) == low, 1.0, 0.0).astype(BF16)
        found = dot_nn(pt[...], low_hot)
        state = jnp.zeros((CH, MIG), F32)
        high_b = jnp.broadcast_to(high, (CH, MIG))
        for g in range(RES):
            state = jnp.where(high_b == g, found[g * CH : (g + 1) * CH], state)
        flag = jnp.where(valid, 1.0, 0.0)
        smig[j, 0:CH] = (state * flag).astype(BF16)
        smig[j, CH : 2 * CH] = jnp.broadcast_to(flag, (CH, MIG)).astype(BF16)
        high_hot = jnp.where(iota((RES, MIG), 0) == high, flag, 0.0).astype(BF16)
        hits = hits + dot_nt(high_hot, low_hot)
    live[0:RES] = 1.0 - hits

    pl.semaphore_wait(barrier, N_GX + N_GY - 2)
    mig = []
    for j, (dx, dy) in enumerate(((1, 0), (-1, 0), (0, 1), (0, -1))):
        copy = pltpu.make_async_remote_copy(
            smig.at[j], rmig.at[j], mig_ss.at[j], mig_rs.at[j],
            device_id=beside(dx, dy), device_id_type=MESH,
        )
        copy.start()
        mig.append(copy)
    for k in range(1, N_GX):
        pl.semaphore_signal(rows_sem, 1, device_id=beside(k, 0), device_id_type=MESH)

    sub = iota((TILES, TILES), 0)
    lane = iota((TILES, TILES), 1)
    size_row = size[...].astype(F32)
    own_row = owner[...].astype(F32)
    start_col = jnp.sum(jnp.where(lane < sub, size_row, 0.0), axis=1, keepdims=True)
    size_col = jnp.sum(jnp.where(lane == sub, size_row, 0.0), axis=1, keepdims=True)
    start_row = jnp.sum(jnp.where(sub < lane, size_col, 0.0), axis=0, keepdims=True)
    own_col = jnp.sum(jnp.where(lane == sub, own_row, 0.0), axis=1, keepdims=True)
    earlier = jnp.where(own_col == own_row, jnp.where(sub < lane, 1.0, 0.0), 0.0)
    rank_row = jnp.sum(earlier, axis=0, keepdims=True)
    rel_row = (((owner[...] - me) * BACK) & (N - 1)).astype(F32)
    base_row = 64.0 * rank_row - start_row
    sub8 = iota((8, TILES), 0)
    values = jnp.where(sub8 == 0, rel_row, jnp.where(sub8 == 1, base_row, 0.0))
    before = jnp.where(iota((8, TILES), 1) == 0, 0.0, pltpu.roll(values, 1, 1))
    steps = (values - before).astype(BF16)

    offs = toff[...]
    off_low = (offs & (FZ - 1)).astype(F32)
    off_high = (offs >> 7).astype(F32)
    sub128 = iota((N, TILES), 0)
    rank_of = (sub128 & 3).astype(F32)
    what = jnp.where(sub128 < 4, off_low, jnp.where(sub128 < 8, off_high, 0.0))
    what = jnp.where(rank_row == rank_of, what, 0.0).astype(BF16)
    rel_hot = jnp.where(sub128.astype(F32) == rel_row, 1.0, 0.0).astype(BF16)
    meta = dot_nt(rel_hot, what)
    for d in range(0, N, 8):
        ext[pl.ds(d * 8 + 4, 8, stride=8), :] = meta[d : d + 8]

    clos_f = clos[...]
    clos_hi = clos_f.astype(BF16)
    clos_lo = (clos_f - clos_hi.astype(F32)).astype(BF16)
    clos2 = jnp.concatenate([clos_hi.astype(F32), clos_lo.astype(F32)], axis=0).astype(BF16)

    sub16 = iota((16, W), 0)

    def prepare(g, dep, state):
        row = jnp.concatenate([cell[pl.ds(2 * g, 1), :], cell[pl.ds(2 * g + 1, 1), :]], axis=1)
        row = row.astype(F32)
        inside = jnp.where(start_col <= row, 1.0, 0.0).astype(BF16)
        found = dot_nn(steps, inside)
        rel = found[0:1]
        place = row + found[1:2]
        hot = jnp.where(iota((W, W), 0).astype(F32) == place, 1.0, 0.0).astype(BF16)
        lall[lax.div(g, PER), :, pl.ds(pl.multiple_of(lax.rem(g, PER) * W, W), W)] = hot
        rel_a[g] = (rel - jnp.where(sub16 >= 8, 1.0, 0.0)).astype(BF16)
        rel_b[g] = (rel - sub16.astype(F32)).astype(BF16)
        keep8[g] = state
        mixed = dot_nn(clos2, dep)
        mixed = mixed[0:8] + mixed[8:16]
        m16s[g] = jnp.concatenate([mixed, mixed], axis=0).astype(BF16)
        den16s[g] = jnp.broadcast_to(dep[0:1].astype(F32), (16, W)).astype(BF16)

    @pl.loop(0, RES)
    def _(g):
        lanes = pl.ds(pl.multiple_of(g * W, W), W)
        state = part[:, lanes]
        prepare(g, (state * live[pl.ds(g, 1), :]).astype(BF16), state[0:8])

    for copy in mig:
        copy.wait_recv()
    for j in range(4):
        for h in range(2):
            g = RES + 2 * j + h
            live[g : g + 1] = rmig[j, CH : 2 * CH, h * W : (h + 1) * W].astype(F32)[0:1]
            state = rmig[j, 0:CH, h * W : (h + 1) * W]
            prepare(g, state, state.astype(F32)[0:8])

    zero16 = jnp.zeros((16, W), BF16)

    def spread(c, first, count, row0):
        for i in range(PER):
            g = c * PER + i
            at = slice(i * W, (i + 1) * W)
            near, m16 = rel_a[g], m16s[g]
            for k in range(count // 2):
                abuf[row0 + k * 16 : row0 + (k + 1) * 16, at] = jnp.where(
                    near == float(first + 2 * k), m16, zero16
                )
            near, den = rel_b[g], den16s[g]
            for k in range(count // 16):
                abuf[row0 + count * 8 + k * 16 : row0 + count * 8 + (k + 1) * 16, at] = jnp.where(
                    near == float(first + 16 * k), den, zero16
                )

    def send_out(rel):
        sb = lax.div(rel, SB)
        pltpu.make_async_remote_copy(
            sendm.at[rel], recvm.at[rel], am_ss.at[sb], am_rs.at[sb],
            device_id=ahead(rel), device_id_type=MESH,
        ).start()

    for block in range(NB):
        rows = slice(block * ND * 8, (block + 1) * ND * 8)
        acc[...] = jnp.zeros(acc.shape, F32)

        @pl.loop(0, CHUNKS)
        def _(c):
            spread(c, block * ND, ND, 0)
            acc[...] += dot_nt(abuf[...], lall[c])

        mixed = acc[0 : ND * 8]
        den = acc[ND * 8 : ND * 9]
        sendm[block * ND : (block + 1) * ND, :, 0:W] = mixed.reshape(ND, 8, W).astype(BF16)
        den_hi = den.astype(BF16).astype(F32)
        den_lo = den - den_hi
        for d in range(0, ND, 8):
            row = (block * ND + d) * 8
            for half in range(2):
                at = slice(half * 128, (half + 1) * 128)
                ext[pl.ds(row + half, 8, stride=8), :] = den_hi[d : d + 8, at]
                ext[pl.ds(row + 2 + half, 8, stride=8), :] = den_lo[d : d + 8, at]
        sendm[block * ND : (block + 1) * ND, :, W : W + EXT] = (
            ext[rows].reshape(ND, 8, EXT).astype(BF16)
        )
        if block == 0:
            recvm[0] = sendm[0]

        if block == 0:
            pl.semaphore_wait(rows_sem, N_GX - 1)

        @pl.loop(1 if block == 0 else block * ND, (block + 1) * ND)
        def _(rel):
            send_out(rel)

    def span(b):
        return pl.ds(1, SB - 1) if b == 0 else pl.ds(b * SB, SB)

    lane_row = iota((1, FZ), 1)
    first_half = lane_row < 64

    def place(b):
        wait_bytes(meta_s.at[pl.ds(b * SB, SB)], meta_sem.at[b])

        @pl.loop(0, SB // UN)
        def _(q):
            for i in range(UN):
                s = b * SB + q * UN + i
                whole = recvm[s, :, 0:W].astype(F32)
                for j in range(4):
                    half = j // 2
                    keep = first_half if j % 2 == 0 else ~first_half
                    shift = (meta_s[s, j] + (0 if j % 2 == 0 else 64)) & (FZ - 1)
                    at = slice(half * FZ, (half + 1) * FZ)
                    tiles[j * N + s] = pltpu.roll(jnp.where(keep, whole[:, at], 0.0), shift, 1)
                    den = ext[pl.ds(s * 8 + half, 1), :] + ext[pl.ds(s * 8 + 2 + half, 1), :]
                    den = jnp.broadcast_to(jnp.where(keep, den, 0.0), (8, FZ))
                    tden[pl.ds(j * N + s, 1), :] = pltpu.roll(den, shift, 1)[0:1]

    for b in range(NSB):
        wait_bytes(recvm.at[span(b)], am_rs.at[b])
        ext[b * SB * 8 : (b + 1) * SB * 8] = (
            recvm[b * SB : (b + 1) * SB, :, W : W + EXT].astype(F32).reshape(SB * 8, EXT)
        )
        meta_v[b * SB : (b + 1) * SB] = ext[pl.ds(b * SB * 8 + 4, SB, stride=8), :].astype(I32)
        pltpu.make_async_copy(
            meta_v.at[pl.ds(b * SB, SB)], meta_s.at[pl.ds(b * SB, SB)], meta_sem.at[b]
        ).start()

        if b > 0:
            place(b - 1)
    place(NSB - 1)

    square = iota((N, N), 0) == iota((N, N), 1)
    meta_f = meta_v[...].astype(F32)
    cols = []
    for j in range(4):
        cols.append(
            jnp.sum(jnp.where(square, meta_f[:, 4 + j : 5 + j], 0.0), axis=0, keepdims=True)
        )
    col_row = jnp.concatenate(cols, axis=1)
    col_hot = jnp.where(iota((FX * FY, 4 * N), 0).astype(F32) == col_row, 1.0, 0.0)
    for r in range(0, DR, 2):
        pair = [tiles2(tiles, r), tiles2(tiles, r + 1)]
        sums = dot_nn(col_hot.astype(BF16), jnp.concatenate(pair, axis=1))
        flat[r * 64 : (r + 1) * 64] = sums[:, 0:FZ]
        flat[(r + 1) * 64 : (r + 2) * 64] = sums[:, FZ : 2 * FZ]
    den = lax.dot_general(
        col_hot, tden[...], (((1,), (0,)), ((), ())),
        precision=lax.Precision.HIGHEST, preferred_element_type=F32,
    )
    for x in range(FX):
        for y in range(FY):
            c = x * FY + y
            gas[x + 1, y + 1, 0:8] = flat[pl.ds(c, 8, stride=64), :]
            gas[x + 1, y + 1, 8:16] = jnp.broadcast_to(den[c : c + 1], (8, FZ))

    def edge(step, far):
        if step == 0:
            return pl.ds(1, 8)
        if far:
            return pl.ds(0 if step > 0 else 9, 1)
        return pl.ds(8 if step > 0 else 1, 1)

    halo = []
    for i, (dx, dy) in enumerate(SIDES):
        copy = pltpu.make_async_remote_copy(
            gas.at[edge(dx, False), edge(dy, False)], gas.at[edge(dx, True), edge(dy, True)],
            halo_ss.at[i], halo_rs.at[i], device_id=beside(dx, dy), device_id_type=MESH,
        )
        copy.start()
        halo.append(copy)
    for copy in halo:
        copy.wait_recv()

    @pl.loop(0, FX // 2)
    def _(x2):
        for odd in range(2):
            x = 2 * x2 + odd
            over_x = [gas[x, y] + 2.0 * gas[x + 1, y] + gas[x + 2, y] for y in range(FY + 2)]
            for y in range(FY):
                smooth = (over_x[y] + 2.0 * over_x[y + 1] + over_x[y + 2]) * (1.0 / 16.0)
                dens = smooth[8:16]
                drag = smooth[0:8] / (1.0 + dens * dens)
                dtmp[x, y * 8 : (y + 1) * 8] = drag

    tile_hot = jnp.concatenate(
        [
            jnp.where(iota((N, FX * FY), 1).astype(F32) == meta_f[:, 4 + j : 5 + j], 1.0, 0.0)
            for j in range(4)
        ],
        axis=0,
    ).astype(BF16)
    drag_rows = dtmp.reshape(FX * FY * 8, FZ)
    for r in range(0, DR, 2):
        pair = [drag_rows[pl.ds(r + k, FX * FY, stride=8), :].astype(BF16) for k in range(2)]
        got = dot_nn(tile_hot, jnp.concatenate(pair, axis=1))
        picked[r * 4 * N : (r + 1) * 4 * N] = got[:, 0:FZ]
        picked[(r + 1) * 4 * N : (r + 2) * 4 * N] = got[:, FZ : 2 * FZ]

    for b in range(NSB):
        @pl.loop(0, SB // UN)
        def _(q):
            for i in range(UN):
                s = b * SB + q * UN + i
                halves = []
                for half in range(2):
                    pair = []
                    for j in (2 * half, 2 * half + 1):
                        shift = ((0 if j % 2 == 0 else 64) - meta_s[s, j]) & (FZ - 1)
                        pair.append(
                            pltpu.roll(picked[pl.ds(j * N + s, 8, stride=4 * N), :], shift, 1)
                        )
                    halves.append(jnp.where(first_half, pair[0], pair[1]))
                sendr[s] = jnp.concatenate(halves, axis=1).astype(BF16)

        if b == 0:
            retm[0] = sendr[0]

        @pl.loop(1 if b == 0 else b * SB, (b + 1) * SB)
        def _(rel):
            pltpu.make_async_remote_copy(
                sendr.at[rel], retm.at[rel], back_ss.at[b], back_rs.at[b],
                device_id=ahead(N - rel), device_id_type=MESH,
            ).start()

    for r in range(DR):
        for x in range(FX):
            drag_o[r, x] = dtmp[x, pl.ds(r, FY, stride=8), :].astype(BF16)

    rows8 = iota((8, W), 0)
    slip = jnp.zeros((8, W), F32)
    for r in range(DR):
        slip = jnp.where(rows8 == r, damp[r], slip)

    def look(g, c, i, first):
        hot = lall[c, :, i * W : (i + 1) * W]
        rel = jnp.broadcast_to(rel_a[g].astype(F32)[0:1], (8, W))
        at = pl.ds(pl.multiple_of(g * W, W), W)
        got = jnp.zeros((8, W), F32) if first == 0 else force_o[:, at]
        for b in range(first, first + NSB // 2):
            full = dot_nn(rbuf[b * SB * 8 : (b + 1) * SB * 8], hot)
            for d in range(SB):
                got = jnp.where(rel == float(b * SB + d), full[d * 8 : (d + 1) * 8], got)
        return at, got

    for first in (0, NSB // 2):
        for b in range(first, first + NSB // 2):
            wait_bytes(retm.at[span(b)], back_rs.at[b])
            back = retm[b * SB : (b + 1) * SB].astype(F32).reshape(SB * 8, W)
            rbuf[b * SB * 8 : (b + 1) * SB * 8] = back.astype(BF16)
        if first == 0:
            @pl.loop(0, CHUNKS)
            def _(c):
                for i in range(PER):
                    at, got = look(c * PER + i, c, i, 0)
                    force_o[:, at] = got
        else:
            @pl.loop(0, CHUNKS)
            def _(c):
                for i in range(PER):
                    g = c * PER + i
                    at, got = look(g, c, i, first)
                    force_o[:, at] = live[pl.ds(g, 1), :] * (got - slip * keep8[g])

    for copy in mig + halo:
        copy.wait_send()
    for b in range(NSB):
        wait_bytes(sendm.at[span(b)], am_ss.at[b])
        wait_bytes(sendr.at[span(b)], back_ss.at[b])


def per_device(
    particles, migrant_index, migrant_count, migrated_slot_cell, source_tile_size,
    tile_owner, tile_offset, closure, damping,
):
    vmem = pl.BlockSpec(memory_space=pltpu.VMEM)
    smem = pl.BlockSpec(memory_space=pltpu.SMEM)
    dma = pltpu.SemaphoreType.DMA
    scratch = [
        pltpu.VMEM((RES * CH, W), BF16),
        pltpu.VMEM((4, 2 * CH, MIG), BF16),
        pltpu.VMEM((4, 2 * CH, MIG), BF16),
        pltpu.VMEM((BLOCKS, W), F32),
        pltpu.VMEM((BLOCKS, 16, W), BF16),
        pltpu.VMEM((BLOCKS, 16, W), BF16),
        pltpu.VMEM((CHUNKS, W, KC), BF16),
        pltpu.VMEM((BLOCKS, 16, W), BF16),
        pltpu.VMEM((BLOCKS, 16, W), BF16),
        pltpu.VMEM((ND * 9, KC), BF16),
        pltpu.VMEM((ND * 9, W), F32),
        pltpu.VMEM((N, 8, W + EXT), BF16),
        pltpu.VMEM((N * 8, EXT), F32),
        pltpu.VMEM((N, 8, W + EXT), BF16),
        pltpu.VMEM((N, 128), I32),
        pltpu.SMEM((N, 128), I32),
        pltpu.VMEM((4 * N, 8, FZ), F32),
        pltpu.VMEM((4 * N, FZ), F32),
        pltpu.VMEM((DR * FX * FY, FZ), F32),
        pltpu.VMEM((DR * 4 * N, FZ), F32),
        pltpu.VMEM((BLOCKS, 8, W), F32),
        pltpu.VMEM((FX + 2, FY + 2, 16, FZ), F32),
        pltpu.VMEM((FX, FY * 8, FZ), F32),
        pltpu.VMEM((N, 8, W), BF16),
        pltpu.VMEM((N, 8, W), BF16),
        pltpu.VMEM((N * 8, W), BF16),
        dma((4,)), dma((4,)), dma((NSB,)), dma((NSB,)),
        dma((8,)), dma((8,)), dma((NSB,)), dma((NSB,)), dma((NSB,)), pltpu.SemaphoreType.REGULAR,
    ]
    return pl.pallas_call(
        body,
        out_shape=(
            jax.ShapeDtypeStruct((DR, FX, FY, FZ), BF16),
            jax.ShapeDtypeStruct((DR, SLOTS), F32),
        ),
        in_specs=[vmem, vmem, smem, vmem, vmem, vmem, vmem, vmem, smem],
        out_specs=(vmem, vmem),
        scratch_shapes=scratch,
        compiler_params=pltpu.CompilerParams(
            collective_id=0, has_side_effects=True, vmem_limit_bytes=60 * 1024 * 1024
        ),
    )(
        particles,
        migrant_index,
        migrant_count,
        migrated_slot_cell.reshape(2 * BLOCKS, 128),
        source_tile_size,
        tile_owner.reshape(1, TILES),
        tile_offset.reshape(1, TILES),
        closure,
        damping,
    )


def solution(mesh):
    in_specs = (
        P(None, ("gx", "gy")),
        P(("gx", "gy"), None),
        P(("gx", "gy"), None),
        P(("gx", "gy")),
        P(("gx", "gy"), None),
        P(("gx", "gy"), None),
        P(("gx", "gy")),
        P(),
        P(),
    )
    out_specs = (P(None, "gx", "gy", None), P(None, ("gx", "gy")))
    return jax.shard_map(
        per_device, mesh=mesh, in_specs=in_specs, out_specs=out_specs, check_vma=False
    )
```

```python
import jax
import jax.numpy as jnp
from jax import lax
from jax.experimental import pallas as pl
from jax.experimental.pallas import tpu as pltpu
from jax.sharding import PartitionSpec as P

F32 = jnp.float32
BF16 = jnp.bfloat16
I32 = jnp.int32
MESH = pl.DeviceIdType.MESH

N_GX = 8
N_GY = 16
N = N_GX * N_GY
CH = 16
DR = 8
PART = 8192
MIG = 512
SLOTS = PART + 4 * MIG
TILES = 256
FX = 8
FY = 8
FZ = 128
W = 256
BLOCKS = SLOTS // W
RES = PART // W
PER = 4
CHUNKS = BLOCKS // PER
KC = PER * W
ND = 64
NB = N // ND
SB = 16
NSB = N // SB
GROUPS = 96
UN = 8
HOP = 21
BACK = 61
EXT = 128
SIDES = tuple((dx, dy) for dx in (-1, 0, 1) for dy in (-1, 0, 1) if dx or dy)


def dot_nn(a, b):
    return lax.dot_general(a, b, (((1,), (0,)), ((), ())), preferred_element_type=F32)


def dot_nt(a, b):
    return lax.dot_general(a, b, (((1,), (1,)), ((), ())), preferred_element_type=F32)


def iota(shape, dim):
    return lax.broadcasted_iota(I32, shape, dim)


def tiles2(tiles, r):
    return tiles.reshape(4 * N * 8, FZ)[pl.ds(r, 4 * N, stride=8), :].astype(BF16)


def wait_bytes(ref, sem):
    pltpu.make_async_copy(ref, ref, sem).wait()


def body(
    part, midx, cnt, cell, size, owner, toff, clos, damp,
    drag_o, force_o,
    pt, smig, rmig, live, rel_a, rel_b, lall, m16s, den16s, abuf, acc,
    sendm, ext, recvm, meta_v, meta_s, tiles, tden, flat, picked, cellv, own_v, own_s, keep8, gas, dtmp, sendr, retm, rbuf,
    mig_ss, mig_rs, am_ss, am_rs, halo_ss, halo_rs, back_ss, back_rs, meta_sem, rows_sem, own_sem,
):
    gx = lax.axis_index("gx")
    gy = lax.axis_index("gy")
    me = gx * N_GY + gy

    def ahead(rel):
        target = (me + rel * HOP) & (N - 1)
        return (target >> 4, target & (N_GY - 1))

    def beside(dx, dy):
        return ((gx + dx) & (N_GX - 1), (gy + dy) & (N_GY - 1))

    barrier = pltpu.get_barrier_semaphore()

    for k in range(1, N_GY):
        pl.semaphore_signal(barrier, 1, device_id=beside(0, k), device_id_type=MESH)
    for k in range(1, N_GX):
        pl.semaphore_signal(barrier, 1, device_id=beside(k, 0), device_id_type=MESH)

    @pl.loop(0, RES)
    def _(g):
        lanes = pl.ds(pl.multiple_of(g * W, W), W)
        pt[pl.ds(pl.multiple_of(g * CH, CH), CH), :] = part[:, lanes].astype(BF16)

    hits = jnp.zeros((RES, W), F32)
    for j in range(4):
        entry = midx[j : j + 1, :]
        low = entry & (W - 1)
        high = entry >> 8
        valid = iota((1, MIG), 1) < cnt[0, j]
        low_hot = jnp.where(iota((W, MIG), 0) == low, 1.0, 0.0).astype(BF16)
        found = dot_nn(pt[...], low_hot)
        state = jnp.zeros((CH, MIG), F32)
        high_b = jnp.broadcast_to(high, (CH, MIG))
        for g in range(RES):
            state = jnp.where(high_b == g, found[g * CH : (g + 1) * CH], state)
        flag = jnp.where(valid, 1.0, 0.0)
        smig[j, 0:CH] = (state * flag).astype(BF16)
        smig[j, CH : 2 * CH] = jnp.broadcast_to(flag, (CH, MIG)).astype(BF16)
        high_hot = jnp.where(iota((RES, MIG), 0) == high, flag, 0.0).astype(BF16)
        hits = hits + dot_nt(high_hot, low_hot)
    live[0:RES] = 1.0 - hits

    pl.semaphore_wait(barrier, N_GX + N_GY - 2)
    mig = []
    for j, (dx, dy) in enumerate(((1, 0), (-1, 0), (0, 1), (0, -1))):
        copy = pltpu.make_async_remote_copy(
            smig.at[j], rmig.at[j], mig_ss.at[j], mig_rs.at[j],
            device_id=beside(dx, dy), device_id_type=MESH,
        )
        copy.start()
        mig.append(copy)
    for k in range(1, N_GX):
        pl.semaphore_signal(rows_sem, 1, device_id=beside(k, 0), device_id_type=MESH)

    sub = iota((TILES, TILES), 0)
    lane = iota((TILES, TILES), 1)
    size_row = size[...].astype(F32)
    own_row = owner[...].astype(F32)
    start_col = jnp.sum(jnp.where(lane < sub, size_row, 0.0), axis=1, keepdims=True)
    size_col = jnp.sum(jnp.where(lane == sub, size_row, 0.0), axis=1, keepdims=True)
    start_row = jnp.sum(jnp.where(sub < lane, size_col, 0.0), axis=0, keepdims=True)
    own_col = jnp.sum(jnp.where(lane == sub, own_row, 0.0), axis=1, keepdims=True)
    earlier = jnp.where(own_col == own_row, jnp.where(sub < lane, 1.0, 0.0), 0.0)
    rank_row = jnp.sum(earlier, axis=0, keepdims=True)
    rel_row = (((owner[...] - me) * BACK) & (N - 1)).astype(F32)
    base_row = 64.0 * rank_row - start_row
    sub8 = iota((8, TILES), 0)
    values = jnp.where(sub8 == 0, rel_row, jnp.where(sub8 == 1, base_row, 0.0))
    before = jnp.where(iota((8, TILES), 1) == 0, 0.0, pltpu.roll(values, 1, 1))
    steps = (values - before).astype(BF16)

    offs = toff[...]
    off_low = (offs & (FZ - 1)).astype(F32)
    off_high = (offs >> 7).astype(F32)
    sub128 = iota((N, TILES), 0)
    rank_of = (sub128 & 3).astype(F32)
    start_int = start_row.astype(I32)
    within = (start_int & 127).astype(F32)
    group = (start_int >> 7).astype(F32)
    what = jnp.where(sub128 < 4, off_low, jnp.where(sub128 < 8, off_high, 0.0))
    what = jnp.where((sub128 >= 8) & (sub128 < 12), within, what)
    what = jnp.where((sub128 >= 12) & (sub128 < 16), group, what)
    what = jnp.where((sub128 >= 16) & (sub128 < 20), size_row, what)
    what = jnp.where(rank_row == rank_of, what, 0.0).astype(BF16)
    rel_hot = jnp.where(sub128.astype(F32) == rel_row, 1.0, 0.0).astype(BF16)
    meta = dot_nt(rel_hot, what)
    own_v[...] = meta.astype(I32)
    own_copy = pltpu.make_async_copy(own_v, own_s, own_sem)
    own_copy.start()
    for d in range(0, N, 8):
        ext[pl.ds(d * 8 + 4, 8, stride=8), :] = meta[d : d + 8]

    clos_f = clos[...]
    clos_hi = clos_f.astype(BF16)
    clos_lo = (clos_f - clos_hi.astype(F32)).astype(BF16)
    clos2 = jnp.concatenate([clos_hi.astype(F32), clos_lo.astype(F32)], axis=0).astype(BF16)

    sub16 = iota((16, W), 0)

    def prepare(g, dep, state):
        row = jnp.concatenate([cell[pl.ds(2 * g, 1), :], cell[pl.ds(2 * g + 1, 1), :]], axis=1)
        row = row.astype(F32)
        inside = jnp.where(start_col <= row, 1.0, 0.0).astype(BF16)
        found = dot_nn(steps, inside)
        rel = found[0:1]
        place = row + found[1:2]
        hot = jnp.where(iota((W, W), 0).astype(F32) == place, 1.0, 0.0).astype(BF16)
        lall[lax.div(g, PER), :, pl.ds(pl.multiple_of(lax.rem(g, PER) * W, W), W)] = hot
        rel_a[g] = (rel - jnp.where(sub16 >= 8, 1.0, 0.0)).astype(BF16)
        rel_b[g] = (rel - sub16.astype(F32)).astype(BF16)
        keep8[g] = state
        mixed = dot_nn(clos2, dep)
        mixed = mixed[0:8] + mixed[8:16]
        m16s[g] = jnp.concatenate([mixed, mixed], axis=0).astype(BF16)
        den16s[g] = jnp.broadcast_to(dep[0:1].astype(F32), (16, W)).astype(BF16)

    @pl.loop(0, RES)
    def _(g):
        lanes = pl.ds(pl.multiple_of(g * W, W), W)
        state = part[:, lanes]
        prepare(g, (state * live[pl.ds(g, 1), :]).astype(BF16), state[0:8])

    for copy in mig:
        copy.wait_recv()
    for j in range(4):
        for h in range(2):
            g = RES + 2 * j + h
            live[g : g + 1] = rmig[j, CH : 2 * CH, h * W : (h + 1) * W].astype(F32)[0:1]
            state = rmig[j, 0:CH, h * W : (h + 1) * W]
            prepare(g, state, state.astype(F32)[0:8])

    zero16 = jnp.zeros((16, W), BF16)

    def spread(c, first, count, row0):
        for i in range(PER):
            g = c * PER + i
            at = slice(i * W, (i + 1) * W)
            near, m16 = rel_a[g], m16s[g]
            for k in range(count // 2):
                abuf[row0 + k * 16 : row0 + (k + 1) * 16, at] = jnp.where(
                    near == float(first + 2 * k), m16, zero16
                )
            near, den = rel_b[g], den16s[g]
            for k in range(count // 16):
                abuf[row0 + count * 8 + k * 16 : row0 + count * 8 + (k + 1) * 16, at] = jnp.where(
                    near == float(first + 16 * k), den, zero16
                )

    def send_out(rel):
        sb = lax.div(rel, SB)
        pltpu.make_async_remote_copy(
            sendm.at[rel], recvm.at[rel], am_ss.at[sb], am_rs.at[sb],
            device_id=ahead(rel), device_id_type=MESH,
        ).start()

    for block in range(NB):
        rows = slice(block * ND * 8, (block + 1) * ND * 8)
        acc[...] = jnp.zeros(acc.shape, F32)

        @pl.loop(0, CHUNKS)
        def _(c):
            spread(c, block * ND, ND, 0)
            acc[...] += dot_nt(abuf[...], lall[c])

        mixed = acc[0 : ND * 8]
        den = acc[ND * 8 : ND * 9]
        sendm[block * ND : (block + 1) * ND, :, 0:W] = mixed.reshape(ND, 8, W).astype(BF16)
        den_hi = den.astype(BF16).astype(F32)
        den_lo = den - den_hi
        for d in range(0, ND, 8):
            row = (block * ND + d) * 8
            for half in range(2):
                at = slice(half * 128, (half + 1) * 128)
                ext[pl.ds(row + half, 8, stride=8), :] = den_hi[d : d + 8, at]
                ext[pl.ds(row + 2 + half, 8, stride=8), :] = den_lo[d : d + 8, at]
        sendm[block * ND : (block + 1) * ND, :, W : W + EXT] = (
            ext[rows].reshape(ND, 8, EXT).astype(BF16)
        )
        if block == 0:
            recvm[0] = sendm[0]

        if block == 0:
            pl.semaphore_wait(rows_sem, N_GX - 1)

        @pl.loop(1 if block == 0 else block * ND, (block + 1) * ND)
        def _(rel):
            send_out(rel)

    def span(b):
        return pl.ds(1, SB - 1) if b == 0 else pl.ds(b * SB, SB)

    lane_row = iota((1, FZ), 1)
    first_half = lane_row < 64

    def place(b):
        wait_bytes(meta_s.at[pl.ds(b * SB, SB)], meta_sem.at[b])

        @pl.loop(0, SB // UN)
        def _(q):
            for i in range(UN):
                s = b * SB + q * UN + i
                whole = recvm[s, :, 0:W].astype(F32)
                for j in range(4):
                    half = j // 2
                    keep = first_half if j % 2 == 0 else ~first_half
                    shift = (meta_s[s, j] + (0 if j % 2 == 0 else 64)) & (FZ - 1)
                    at = slice(half * FZ, (half + 1) * FZ)
                    tiles[j * N + s] = pltpu.roll(jnp.where(keep, whole[:, at], 0.0), shift, 1)
                    den = ext[pl.ds(s * 8 + half, 1), :] + ext[pl.ds(s * 8 + 2 + half, 1), :]
                    den = jnp.broadcast_to(jnp.where(keep, den, 0.0), (8, FZ))
                    tden[pl.ds(j * N + s, 1), :] = pltpu.roll(den, shift, 1)[0:1]

    for b in range(NSB):
        wait_bytes(recvm.at[span(b)], am_rs.at[b])
        ext[b * SB * 8 : (b + 1) * SB * 8] = (
            recvm[b * SB : (b + 1) * SB, :, W : W + EXT].astype(F32).reshape(SB * 8, EXT)
        )
        meta_v[b * SB : (b + 1) * SB] = ext[pl.ds(b * SB * 8 + 4, SB, stride=8), :].astype(I32)
        pltpu.make_async_copy(
            meta_v.at[pl.ds(b * SB, SB)], meta_s.at[pl.ds(b * SB, SB)], meta_sem.at[b]
        ).start()

        if b > 0:
            place(b - 1)
    place(NSB - 1)

    square = iota((N, N), 0) == iota((N, N), 1)
    meta_f = meta_v[...].astype(F32)
    cols = []
    for j in range(4):
        cols.append(
            jnp.sum(jnp.where(square, meta_f[:, 4 + j : 5 + j], 0.0), axis=0, keepdims=True)
        )
    col_row = jnp.concatenate(cols, axis=1)
    col_hot = jnp.where(iota((FX * FY, 4 * N), 0).astype(F32) == col_row, 1.0, 0.0)
    for r in range(0, DR, 2):
        pair = [tiles2(tiles, r), tiles2(tiles, r + 1)]
        sums = dot_nn(col_hot.astype(BF16), jnp.concatenate(pair, axis=1))
        flat[r * 64 : (r + 1) * 64] = sums[:, 0:FZ]
        flat[(r + 1) * 64 : (r + 2) * 64] = sums[:, FZ : 2 * FZ]
    den = lax.dot_general(
        col_hot, tden[...], (((1,), (0,)), ((), ())),
        precision=lax.Precision.HIGHEST, preferred_element_type=F32,
    )
    for x in range(FX):
        for y in range(FY):
            c = x * FY + y
            gas[x + 1, y + 1, 0:8] = flat[pl.ds(c, 8, stride=64), :]
            gas[x + 1, y + 1, 8:16] = jnp.broadcast_to(den[c : c + 1], (8, FZ))

    def edge(step, far):
        if step == 0:
            return pl.ds(1, 8)
        if far:
            return pl.ds(0 if step > 0 else 9, 1)
        return pl.ds(8 if step > 0 else 1, 1)

    halo = []
    for i, (dx, dy) in enumerate(SIDES):
        copy = pltpu.make_async_remote_copy(
            gas.at[edge(dx, False), edge(dy, False)], gas.at[edge(dx, True), edge(dy, True)],
            halo_ss.at[i], halo_rs.at[i], device_id=beside(dx, dy), device_id_type=MESH,
        )
        copy.start()
        halo.append(copy)
    for copy in halo:
        copy.wait_recv()

    @pl.loop(0, FX // 2)
    def _(x2):
        for odd in range(2):
            x = 2 * x2 + odd
            over_x = [gas[x, y] + 2.0 * gas[x + 1, y] + gas[x + 2, y] for y in range(FY + 2)]
            for y in range(FY):
                smooth = (over_x[y] + 2.0 * over_x[y + 1] + over_x[y + 2]) * (1.0 / 16.0)
                dens = smooth[8:16]
                drag = smooth[0:8] / (1.0 + dens * dens)
                dtmp[x, y * 8 : (y + 1) * 8] = drag

    tile_hot = jnp.concatenate(
        [
            jnp.where(iota((N, FX * FY), 1).astype(F32) == meta_f[:, 4 + j : 5 + j], 1.0, 0.0)
            for j in range(4)
        ],
        axis=0,
    ).astype(BF16)
    drag_rows = dtmp.reshape(FX * FY * 8, FZ)
    for r in range(0, DR, 2):
        pair = [drag_rows[pl.ds(r + k, FX * FY, stride=8), :].astype(BF16) for k in range(2)]
        got = dot_nn(tile_hot, jnp.concatenate(pair, axis=1))
        picked[r * 4 * N : (r + 1) * 4 * N] = got[:, 0:FZ]
        picked[(r + 1) * 4 * N : (r + 2) * 4 * N] = got[:, FZ : 2 * FZ]

    for b in range(NSB):
        @pl.loop(0, SB // UN)
        def _(q):
            for i in range(UN):
                s = b * SB + q * UN + i
                halves = []
                for half in range(2):
                    pair = []
                    for j in (2 * half, 2 * half + 1):
                        shift = ((0 if j % 2 == 0 else 64) - meta_s[s, j]) & (FZ - 1)
                        pair.append(
                            pltpu.roll(picked[pl.ds(j * N + s, 8, stride=4 * N), :], shift, 1)
                        )
                    halves.append(jnp.where(first_half, pair[0], pair[1]))
                sendr[s] = jnp.concatenate(halves, axis=1).astype(BF16)

        if b == 0:
            retm[0] = sendr[0]

        @pl.loop(1 if b == 0 else b * SB, (b + 1) * SB)
        def _(rel):
            pltpu.make_async_remote_copy(
                sendr.at[rel], retm.at[rel], back_ss.at[b], back_rs.at[b],
                device_id=ahead(N - rel), device_id_type=MESH,
            ).start()

    for r in range(DR):
        for x in range(FX):
            drag_o[r, x] = dtmp[x, pl.ds(r, FY, stride=8), :].astype(BF16)

    rows8 = iota((8, W), 0)
    slip = jnp.zeros((8, W), F32)
    for r in range(DR):
        slip = jnp.where(rows8 == r, damp[r], slip)

    own_copy.wait()
    lanes = iota((8, FZ), 1)
    own_f = own_v[...].astype(F32)
    group_row = jnp.concatenate(
        [
            jnp.sum(jnp.where(square, own_f[:, 12 + j : 13 + j], 0.0), axis=0, keepdims=True)
            for j in range(4)
        ],
        axis=1,
    )
    group_ids = iota((GROUPS, 4 * N), 0).astype(F32)
    group_hot = jnp.concatenate(
        [
            jnp.where(group_ids == group_row, 1.0, 0.0),
            jnp.where(group_ids == group_row + 1.0, 1.0, 0.0),
        ],
        axis=1,
    ).astype(BF16)
    begins = jnp.concatenate([own_f[:, 8 + j : 9 + j] for j in range(4)], axis=0)
    here = jnp.where(iota((4 * N, FZ), 1).astype(F32) >= begins, 1.0, 0.0).astype(BF16)
    after = (1.0 - here.astype(F32)).astype(BF16)

    @pl.loop(0, CHUNKS)
    def _(c):
        for i in range(PER):
            g = c * PER + i
            row = jnp.concatenate([cell[pl.ds(2 * g, 1), :], cell[pl.ds(2 * g + 1, 1), :]], axis=1)
            lall[c, :, i * W : (i + 1) * W] = jnp.where(
                iota((W, W), 0) == (row & (W - 1)), 1.0, 0.0
            ).astype(BF16)

    for b in range(NSB):
        wait_bytes(retm.at[span(b)], back_rs.at[b])

        @pl.loop(0, SB // UN)
        def _(q):
            for i in range(UN):
                s = b * SB + q * UN + i
                whole = retm[s].astype(F32)
                for j in range(4):
                    half, base = j // 2, 64 * (j % 2)
                    count = own_s[s, 16 + j]
                    keep = (lanes >= base) & (lanes < base + count)
                    value = jnp.where(keep, whole[:, half * FZ : (half + 1) * FZ], 0.0)
                    shift = (own_s[s, 8 + j] - base) & (FZ - 1)
                    tiles[j * N + s] = pltpu.roll(value, shift, 1)

    for r in range(0, DR, 2):
        pair = []
        for k in range(2):
            rows = tiles2(tiles, r + k)
            pair.append(jnp.concatenate([rows * here, rows * after], axis=0))
        got = dot_nn(group_hot, jnp.concatenate(pair, axis=1))
        cellv[r * GROUPS : (r + 1) * GROUPS] = got[:, 0:FZ]
        cellv[(r + 1) * GROUPS : (r + 2) * GROUPS] = got[:, FZ : 2 * FZ]
    for h in range(0, GROUPS // 2, 2):
        both = []
        for k in range(2):
            first = 2 * (h + k)
            both.append(
                jnp.concatenate(
                    [
                        cellv[pl.ds(first, 8, stride=GROUPS), :],
                        cellv[pl.ds(first + 1, 8, stride=GROUPS), :],
                    ],
                    axis=1,
                )
            )
        rbuf[h * 8 : (h + 2) * 8] = jnp.concatenate(both, axis=0).astype(BF16)

    @pl.loop(0, CHUNKS)
    def _(c):
        for i in range(PER):
            g = c * PER + i
            row = jnp.concatenate([cell[pl.ds(2 * g, 1), :], cell[pl.ds(2 * g + 1, 1), :]], axis=1)
            high = jnp.broadcast_to(row >> 8, (8, W))
            full = dot_nn(rbuf[...], lall[c, :, i * W : (i + 1) * W])
            got = jnp.zeros((8, W), F32)
            for h in range(GROUPS // 2):
                got = jnp.where(high == h, full[h * 8 : (h + 1) * 8], got)
            force_o[:, pl.ds(pl.multiple_of(g * W, W), W)] = live[pl.ds(g, 1), :] * (
                got - slip * keep8[g]
            )

    for copy in mig + halo:
        copy.wait_send()
    for b in range(NSB):
        wait_bytes(sendm.at[span(b)], am_ss.at[b])
        wait_bytes(sendr.at[span(b)], back_ss.at[b])


def per_device(
    particles, migrant_index, migrant_count, migrated_slot_cell, source_tile_size,
    tile_owner, tile_offset, closure, damping,
):
    vmem = pl.BlockSpec(memory_space=pltpu.VMEM)
    smem = pl.BlockSpec(memory_space=pltpu.SMEM)
    dma = pltpu.SemaphoreType.DMA
    scratch = [
        pltpu.VMEM((RES * CH, W), BF16),
        pltpu.VMEM((4, 2 * CH, MIG), BF16),
        pltpu.VMEM((4, 2 * CH, MIG), BF16),
        pltpu.VMEM((BLOCKS, W), F32),
        pltpu.VMEM((BLOCKS, 16, W), BF16),
        pltpu.VMEM((BLOCKS, 16, W), BF16),
        pltpu.VMEM((CHUNKS, W, KC), BF16),
        pltpu.VMEM((BLOCKS, 16, W), BF16),
        pltpu.VMEM((BLOCKS, 16, W), BF16),
        pltpu.VMEM((ND * 9, KC), BF16),
        pltpu.VMEM((ND * 9, W), F32),
        pltpu.VMEM((N, 8, W + EXT), BF16),
        pltpu.VMEM((N * 8, EXT), F32),
        pltpu.VMEM((N, 8, W + EXT), BF16),
        pltpu.VMEM((N, 128), I32),
        pltpu.SMEM((N, 128), I32),
        pltpu.VMEM((4 * N, 8, FZ), F32),
        pltpu.VMEM((4 * N, FZ), F32),
        pltpu.VMEM((DR * FX * FY, FZ), F32),
        pltpu.VMEM((DR * 4 * N, FZ), F32),
        pltpu.VMEM((DR * GROUPS, FZ), F32),
        pltpu.VMEM((N, 128), I32),
        pltpu.SMEM((N, 128), I32),
        pltpu.VMEM((BLOCKS, 8, W), F32),
        pltpu.VMEM((FX + 2, FY + 2, 16, FZ), F32),
        pltpu.VMEM((FX, FY * 8, FZ), F32),
        pltpu.VMEM((N, 8, W), BF16),
        pltpu.VMEM((N, 8, W), BF16),
        pltpu.VMEM((GROUPS * 4, W), BF16),
        dma((4,)), dma((4,)), dma((NSB,)), dma((NSB,)),
        dma((8,)), dma((8,)), dma((NSB,)), dma((NSB,)), dma((NSB,)), pltpu.SemaphoreType.REGULAR, dma(()),
    ]
    return pl.pallas_call(
        body,
        out_shape=(
            jax.ShapeDtypeStruct((DR, FX, FY, FZ), BF16),
            jax.ShapeDtypeStruct((DR, SLOTS), F32),
        ),
        in_specs=[vmem, vmem, smem, vmem, vmem, vmem, vmem, vmem, smem],
        out_specs=(vmem, vmem),
        scratch_shapes=scratch,
        compiler_params=pltpu.CompilerParams(
            collective_id=0, has_side_effects=True, vmem_limit_bytes=60 * 1024 * 1024
        ),
    )(
        particles,
        migrant_index,
        migrant_count,
        migrated_slot_cell.reshape(2 * BLOCKS, 128),
        source_tile_size,
        tile_owner.reshape(1, TILES),
        tile_offset.reshape(1, TILES),
        closure,
        damping,
    )


def solution(mesh):
    in_specs = (
        P(None, ("gx", "gy")),
        P(("gx", "gy"), None),
        P(("gx", "gy"), None),
        P(("gx", "gy")),
        P(("gx", "gy"), None),
        P(("gx", "gy"), None),
        P(("gx", "gy")),
        P(),
        P(),
    )
    out_specs = (P(None, "gx", "gy", None), P(None, ("gx", "gy")))
    return jax.shard_map(
        per_device, mesh=mesh, in_specs=in_specs, out_specs=out_specs, check_vma=False
    )
```

```python
import jax
import jax.numpy as jnp
from jax import lax
from jax.experimental import pallas as pl
from jax.experimental.pallas import tpu as pltpu
from jax.sharding import PartitionSpec as P

F32 = jnp.float32
BF16 = jnp.bfloat16
I32 = jnp.int32
MESH = pl.DeviceIdType.MESH

N_GX = 8
N_GY = 16
N = N_GX * N_GY
CH = 16
DR = 8
PART = 8192
MIG = 512
SLOTS = PART + 4 * MIG
TILES = 256
FX = 8
FY = 8
FZ = 128
W = 256
BLOCKS = SLOTS // W
RES = PART // W
PER = 4
CHUNKS = BLOCKS // PER
KC = PER * W
SB = 16
NSB = N // SB
GROUPS = 96
UN = 8
HOP = 21
BACK = 61
EXT = 128
SIDES = tuple((dx, dy) for dx in (-1, 0, 1) for dy in (-1, 0, 1) if dx or dy)


def dot_nn(a, b):
    return lax.dot_general(a, b, (((1,), (0,)), ((), ())), preferred_element_type=F32)


def dot_nt(a, b):
    return lax.dot_general(a, b, (((1,), (1,)), ((), ())), preferred_element_type=F32)


def iota(shape, dim):
    return lax.broadcasted_iota(I32, shape, dim)


def tiles2(tiles, r):
    return tiles.reshape(4 * N * 8, FZ)[pl.ds(r, 4 * N, stride=8), :].astype(BF16)


def wait_bytes(ref, sem):
    pltpu.make_async_copy(ref, ref, sem).wait()


def body(
    part, midx, cnt, cell, size, owner, toff, clos, damp,
    drag_o, force_o,
    pt, smig, rmig, live, rel_a, rel_b, lall, m16s, den16s, abuf, acc,
    sendm, ext, recvm, meta_v, meta_s, tiles, tden, flat, picked, cellv, own_v, own_s, keep8, gas, dtmp, sendr, retm, rbuf,
    mig_ss, mig_rs, am_ss, am_rs, halo_ss, halo_rs, back_ss, back_rs, meta_sem, rows_sem, own_sem,
):
    gx = lax.axis_index("gx")
    gy = lax.axis_index("gy")
    me = gx * N_GY + gy

    def ahead(rel):
        target = (me + rel * HOP) & (N - 1)
        return (target >> 4, target & (N_GY - 1))

    def beside(dx, dy):
        return ((gx + dx) & (N_GX - 1), (gy + dy) & (N_GY - 1))

    barrier = pltpu.get_barrier_semaphore()

    for k in range(1, N_GY):
        pl.semaphore_signal(barrier, 1, device_id=beside(0, k), device_id_type=MESH)
    for k in range(1, N_GX):
        pl.semaphore_signal(barrier, 1, device_id=beside(k, 0), device_id_type=MESH)

    @pl.loop(0, RES)
    def _(g):
        lanes = pl.ds(pl.multiple_of(g * W, W), W)
        pt[pl.ds(pl.multiple_of(g * CH, CH), CH), :] = part[:, lanes].astype(BF16)

    hits = jnp.zeros((RES, W), F32)
    for j in range(4):
        entry = midx[j : j + 1, :]
        low = entry & (W - 1)
        high = entry >> 8
        valid = iota((1, MIG), 1) < cnt[0, j]
        low_hot = jnp.where(iota((W, MIG), 0) == low, 1.0, 0.0).astype(BF16)
        found = dot_nn(pt[...], low_hot)
        state = jnp.zeros((CH, MIG), F32)
        high_b = jnp.broadcast_to(high, (CH, MIG))
        for g in range(RES):
            state = jnp.where(high_b == g, found[g * CH : (g + 1) * CH], state)
        flag = jnp.where(valid, 1.0, 0.0)
        smig[j, 0:CH] = (state * flag).astype(BF16)
        smig[j, CH : 2 * CH] = jnp.broadcast_to(flag, (CH, MIG)).astype(BF16)
        high_hot = jnp.where(iota((RES, MIG), 0) == high, flag, 0.0).astype(BF16)
        hits = hits + dot_nt(high_hot, low_hot)
    live[0:RES] = 1.0 - hits

    pl.semaphore_wait(barrier, N_GX + N_GY - 2)
    mig = []
    for j, (dx, dy) in enumerate(((1, 0), (-1, 0), (0, 1), (0, -1))):
        copy = pltpu.make_async_remote_copy(
            smig.at[j], rmig.at[j], mig_ss.at[j], mig_rs.at[j],
            device_id=beside(dx, dy), device_id_type=MESH,
        )
        copy.start()
        mig.append(copy)
    for k in range(1, N_GX):
        pl.semaphore_signal(rows_sem, 1, device_id=beside(k, 0), device_id_type=MESH)

    sub = iota((TILES, TILES), 0)
    lane = iota((TILES, TILES), 1)
    size_row = size[...].astype(F32)
    own_row = owner[...].astype(F32)
    size_col = jnp.sum(jnp.where(lane == sub, size_row, 0.0), axis=1, keepdims=True)
    start_row = jnp.sum(jnp.where(sub < lane, size_col, 0.0), axis=0, keepdims=True)
    own_col = jnp.sum(jnp.where(lane == sub, own_row, 0.0), axis=1, keepdims=True)
    earlier = jnp.where(own_col == own_row, jnp.where(sub < lane, 1.0, 0.0), 0.0)
    rank_row = jnp.sum(earlier, axis=0, keepdims=True)
    rel_row = (((owner[...] - me) * BACK) & (N - 1)).astype(F32)
    offs = toff[...]
    off_low = (offs & (FZ - 1)).astype(F32)
    off_high = (offs >> 7).astype(F32)
    sub128 = iota((N, TILES), 0)
    rank_of = (sub128 & 3).astype(F32)
    start_int = start_row.astype(I32)
    within = (start_int & 127).astype(F32)
    group = (start_int >> 7).astype(F32)
    what = jnp.where(sub128 < 4, off_low, jnp.where(sub128 < 8, off_high, 0.0))
    what = jnp.where((sub128 >= 8) & (sub128 < 12), within, what)
    what = jnp.where((sub128 >= 12) & (sub128 < 16), group, what)
    what = jnp.where((sub128 >= 16) & (sub128 < 20), size_row, what)
    what = jnp.where(rank_row == rank_of, what, 0.0).astype(BF16)
    rel_hot = jnp.where(sub128.astype(F32) == rel_row, 1.0, 0.0).astype(BF16)
    meta = dot_nt(rel_hot, what)
    own_v[...] = meta.astype(I32)
    own_copy = pltpu.make_async_copy(own_v, own_s, own_sem)
    own_copy.start()
    clos_f = clos[...]
    clos_hi = clos_f.astype(BF16)
    clos_lo = (clos_f - clos_hi.astype(F32)).astype(BF16)
    clos2 = jnp.concatenate([clos_hi.astype(F32), clos_lo.astype(F32)], axis=0).astype(BF16)

    sub16 = iota((16, W), 0)

    def prepare(g, dep, state):
        row = jnp.concatenate([cell[pl.ds(2 * g, 1), :], cell[pl.ds(2 * g + 1, 1), :]], axis=1)
        hot = jnp.where(iota((W, W), 0) == (row & (W - 1)), 1.0, 0.0).astype(BF16)
        lall[lax.div(g, PER), :, pl.ds(pl.multiple_of(lax.rem(g, PER) * W, W), W)] = hot
        near = (row >> 8) - jnp.zeros((16, W), I32)
        rel_a[g] = (near - jnp.where(sub16 >= 8, 1, 0)).astype(F32).astype(BF16)
        rel_b[g] = (near - sub16).astype(F32).astype(BF16)
        keep8[g] = state
        mixed = dot_nn(clos2, dep)
        mixed = mixed[0:8] + mixed[8:16]
        m16s[g] = jnp.concatenate([mixed, mixed], axis=0).astype(BF16)
        den16s[g] = jnp.broadcast_to(dep[0:1].astype(F32), (16, W)).astype(BF16)

    @pl.loop(0, RES)
    def _(g):
        lanes = pl.ds(pl.multiple_of(g * W, W), W)
        state = part[:, lanes]
        prepare(g, (state * live[pl.ds(g, 1), :]).astype(BF16), state[0:8])

    zero16 = jnp.zeros((16, W), BF16)

    def spread(c, first, count, row0):
        for i in range(PER):
            g = c * PER + i
            at = slice(i * W, (i + 1) * W)
            near, m16 = rel_a[g], m16s[g]
            for k in range(count // 2):
                abuf[row0 + k * 16 : row0 + (k + 1) * 16, at] = jnp.where(
                    near == float(first + 2 * k), m16, zero16
                )
            near, den = rel_b[g], den16s[g]
            for k in range(count // 16):
                abuf[row0 + count * 8 + k * 16 : row0 + count * 8 + (k + 1) * 16, at] = jnp.where(
                    near == float(first + 16 * k), den, zero16
                )

    def send_out(rel):
        sb = lax.div(rel, SB)
        pltpu.make_async_remote_copy(
            sendm.at[rel], recvm.at[rel], am_ss.at[sb], am_rs.at[sb],
            device_id=ahead(rel), device_id_type=MESH,
        ).start()

    acc[...] = jnp.zeros(acc.shape, F32)

    @pl.loop(0, RES // PER)
    def _(c):
        spread(c, 0, GROUPS // 2, 0)
        more = dot_nt(abuf[...], lall[c])
        acc[0] += more[:, 0:FZ]
        acc[1] += more[:, FZ : 2 * FZ]

    for copy in mig:
        copy.wait_recv()
    for j in range(4):
        for h in range(2):
            g = RES + 2 * j + h
            live[g : g + 1] = rmig[j, CH : 2 * CH, h * W : (h + 1) * W].astype(F32)[0:1]
            state = rmig[j, 0:CH, h * W : (h + 1) * W]
            prepare(g, state, state.astype(F32)[0:8])

    @pl.loop(RES // PER, CHUNKS)
    def _(c):
        spread(c, 0, GROUPS // 2, 0)
        more = dot_nt(abuf[...], lall[c])
        acc[0] += more[:, 0:FZ]
        acc[1] += more[:, FZ : 2 * FZ]

    own_copy.wait()
    own_f = own_v[...].astype(F32)
    begins = jnp.concatenate([own_f[:, 8 + j : 9 + j] for j in range(4)], axis=0)
    here_f = jnp.where(iota((4 * N, FZ), 1).astype(F32) >= begins, 1.0, 0.0)

    def group_cols(step):
        hots = []
        for j in range(4):
            col = own_v[:, 12 + j : 13 + j] + step
            col = (col & 1) * (GROUPS // 2) + (col >> 1)
            hots.append(jnp.where(iota((N, GROUPS), 1) == col, 1.0, 0.0))
        return jnp.concatenate(hots, axis=0)

    hot_a, hot_b = group_cols(0), group_cols(1)
    hot_a16, hot_b16 = hot_a.astype(BF16), hot_b.astype(BF16)

    def cells_of(ref_row, stride):
        return jnp.concatenate(
            [acc_at(ref_row, stride, 0), acc_at(ref_row, stride, 1)], axis=0
        )

    def acc_at(first, stride, odd):
        if stride == 1:
            return acc[odd, first : first + GROUPS // 2]
        return acc[odd, pl.ds(first, GROUPS // 2, stride=stride), :]

    for r in range(0, DR, 2):
        pair = jnp.concatenate([cells_of(r, 8), cells_of(r + 1, 8)], axis=1).astype(BF16)
        low_part, high_part = dot_nn(hot_a16, pair), dot_nn(hot_b16, pair)
        for k in range(2):
            at = slice(k * FZ, (k + 1) * FZ)
            picked[(r + k) * 4 * N : (r + k + 1) * 4 * N] = jnp.where(
                here_f > 0.0, low_part[:, at], high_part[:, at]
            )
    den = cells_of(GROUPS * 4, 1)
    den_hi = den.astype(BF16)
    den_lo = (den - den_hi.astype(F32)).astype(BF16)
    den2 = jnp.concatenate([den_hi.astype(F32), den_lo.astype(F32)], axis=1).astype(BF16)
    low_part, high_part = dot_nn(hot_a16, den2), dot_nn(hot_b16, den2)
    tden[...] = jnp.where(
        here_f > 0.0,
        low_part[:, 0:FZ] + low_part[:, FZ : 2 * FZ],
        high_part[:, 0:FZ] + high_part[:, FZ : 2 * FZ],
    )

    pl.semaphore_wait(rows_sem, N_GX - 1)
    slot_lanes = iota((8, FZ), 1)
    slot_rows = iota((8, FZ), 0)
    for b in range(NSB):
        @pl.loop(0, SB // UN)
        def _(q):
            for i in range(UN):
                s = b * SB + q * UN + i
                halves, dens = [], []
                for half in range(2):
                    total = jnp.zeros((8, FZ), F32)
                    dtotal = jnp.zeros((8, FZ), F32)
                    for j in (2 * half, 2 * half + 1):
                        base = 64 * (j % 2)
                        count = own_s[s, 16 + j]
                        shift = (base - own_s[s, 8 + j]) & (FZ - 1)
                        keep = (slot_lanes >= base) & (slot_lanes < base + count)
                        value = picked[pl.ds(j * N + s, 8, stride=4 * N), :]
                        total = jnp.where(keep, pltpu.roll(value, shift, 1), total)
                        dval = jnp.broadcast_to(tden[pl.ds(j * N + s, 1), :], (8, FZ))
                        dtotal = jnp.where(keep, pltpu.roll(dval, shift, 1), dtotal)
                    halves.append(total)
                    dens.append(dtotal)
                sendm[s, :, 0:W] = jnp.concatenate(halves, axis=1).astype(BF16)
                value = jnp.where((slot_rows & 1) == 0, dens[0], dens[1])
                top = value.astype(BF16).astype(F32)
                note = jnp.broadcast_to(own_v[pl.ds(s, 1), :].astype(F32), (8, FZ))
                extra = jnp.where(
                    slot_rows < 2, top, jnp.where(slot_rows < 4, value - top, note)
                )
                sendm[s, :, W : W + EXT] = extra.astype(BF16)

        if b == 0:
            recvm[0] = sendm[0]

        @pl.loop(1 if b == 0 else b * SB, (b + 1) * SB)
        def _(rel):
            send_out(rel)

    def span(b):
        return pl.ds(1, SB - 1) if b == 0 else pl.ds(b * SB, SB)

    lane_row = iota((1, FZ), 1)
    first_half = lane_row < 64

    def place(b):
        wait_bytes(meta_s.at[pl.ds(b * SB, SB)], meta_sem.at[b])

        @pl.loop(0, SB // UN)
        def _(q):
            for i in range(UN):
                s = b * SB + q * UN + i
                whole = recvm[s, :, 0:W].astype(F32)
                for j in range(4):
                    half = j // 2
                    keep = first_half if j % 2 == 0 else ~first_half
                    shift = (meta_s[s, j] + (0 if j % 2 == 0 else 64)) & (FZ - 1)
                    at = slice(half * FZ, (half + 1) * FZ)
                    tiles[j * N + s] = pltpu.roll(jnp.where(keep, whole[:, at], 0.0), shift, 1)
                    den = ext[pl.ds(s * 8 + half, 1), :] + ext[pl.ds(s * 8 + 2 + half, 1), :]
                    den = jnp.broadcast_to(jnp.where(keep, den, 0.0), (8, FZ))
                    tden[pl.ds(j * N + s, 1), :] = pltpu.roll(den, shift, 1)[0:1]

    for b in range(NSB):
        wait_bytes(recvm.at[span(b)], am_rs.at[b])
        ext[b * SB * 8 : (b + 1) * SB * 8] = (
            recvm[b * SB : (b + 1) * SB, :, W : W + EXT].astype(F32).reshape(SB * 8, EXT)
        )
        meta_v[b * SB : (b + 1) * SB] = ext[pl.ds(b * SB * 8 + 4, SB, stride=8), :].astype(I32)
        pltpu.make_async_copy(
            meta_v.at[pl.ds(b * SB, SB)], meta_s.at[pl.ds(b * SB, SB)], meta_sem.at[b]
        ).start()

        if b > 0:
            place(b - 1)
    place(NSB - 1)

    square = iota((N, N), 0) == iota((N, N), 1)
    meta_f = meta_v[...].astype(F32)
    cols = []
    for j in range(4):
        cols.append(
            jnp.sum(jnp.where(square, meta_f[:, 4 + j : 5 + j], 0.0), axis=0, keepdims=True)
        )
    col_row = jnp.concatenate(cols, axis=1)
    col_hot = jnp.where(iota((FX * FY, 4 * N), 0).astype(F32) == col_row, 1.0, 0.0)
    for r in range(0, DR, 2):
        pair = [tiles2(tiles, r), tiles2(tiles, r + 1)]
        sums = dot_nn(col_hot.astype(BF16), jnp.concatenate(pair, axis=1))
        flat[r * 64 : (r + 1) * 64] = sums[:, 0:FZ]
        flat[(r + 1) * 64 : (r + 2) * 64] = sums[:, FZ : 2 * FZ]
    den = lax.dot_general(
        col_hot, tden[...], (((1,), (0,)), ((), ())),
        precision=lax.Precision.HIGHEST, preferred_element_type=F32,
    )
    for x in range(FX):
        for y in range(FY):
            c = x * FY + y
            gas[x + 1, y + 1, 0:8] = flat[pl.ds(c, 8, stride=64), :]
            gas[x + 1, y + 1, 8:16] = jnp.broadcast_to(den[c : c + 1], (8, FZ))

    def edge(step, far):
        if step == 0:
            return pl.ds(1, 8)
        if far:
            return pl.ds(0 if step > 0 else 9, 1)
        return pl.ds(8 if step > 0 else 1, 1)

    halo = []
    for i, (dx, dy) in enumerate(SIDES):
        copy = pltpu.make_async_remote_copy(
            gas.at[edge(dx, False), edge(dy, False)], gas.at[edge(dx, True), edge(dy, True)],
            halo_ss.at[i], halo_rs.at[i], device_id=beside(dx, dy), device_id_type=MESH,
        )
        copy.start()
        halo.append(copy)
    for copy in halo:
        copy.wait_recv()

    @pl.loop(0, FX // 2)
    def _(x2):
        for odd in range(2):
            x = 2 * x2 + odd
            over_x = [gas[x, y] + 2.0 * gas[x + 1, y] + gas[x + 2, y] for y in range(FY + 2)]
            for y in range(FY):
                smooth = (over_x[y] + 2.0 * over_x[y + 1] + over_x[y + 2]) * (1.0 / 16.0)
                dens = smooth[8:16]
                drag = smooth[0:8] / (1.0 + dens * dens)
                dtmp[x, y * 8 : (y + 1) * 8] = drag

    tile_hot = jnp.concatenate(
        [
            jnp.where(iota((N, FX * FY), 1).astype(F32) == meta_f[:, 4 + j : 5 + j], 1.0, 0.0)
            for j in range(4)
        ],
        axis=0,
    ).astype(BF16)
    drag_rows = dtmp.reshape(FX * FY * 8, FZ)
    for r in range(0, DR, 2):
        pair = [drag_rows[pl.ds(r + k, FX * FY, stride=8), :].astype(BF16) for k in range(2)]
        got = dot_nn(tile_hot, jnp.concatenate(pair, axis=1))
        picked[r * 4 * N : (r + 1) * 4 * N] = got[:, 0:FZ]
        picked[(r + 1) * 4 * N : (r + 2) * 4 * N] = got[:, FZ : 2 * FZ]

    for b in range(NSB):
        @pl.loop(0, SB // UN)
        def _(q):
            for i in range(UN):
                s = b * SB + q * UN + i
                halves = []
                for half in range(2):
                    pair = []
                    for j in (2 * half, 2 * half + 1):
                        shift = ((0 if j % 2 == 0 else 64) - meta_s[s, j]) & (FZ - 1)
                        pair.append(
                            pltpu.roll(picked[pl.ds(j * N + s, 8, stride=4 * N), :], shift, 1)
                        )
                    halves.append(jnp.where(first_half, pair[0], pair[1]))
                sendr[s] = jnp.concatenate(halves, axis=1).astype(BF16)

        if b == 0:
            retm[0] = sendr[0]

        @pl.loop(1 if b == 0 else b * SB, (b + 1) * SB)
        def _(rel):
            pltpu.make_async_remote_copy(
                sendr.at[rel], retm.at[rel], back_ss.at[b], back_rs.at[b],
                device_id=ahead(N - rel), device_id_type=MESH,
            ).start()

    for r in range(DR):
        for x in range(FX):
            drag_o[r, x] = dtmp[x, pl.ds(r, FY, stride=8), :].astype(BF16)

    rows8 = iota((8, W), 0)
    slip = jnp.zeros((8, W), F32)
    for r in range(DR):
        slip = jnp.where(rows8 == r, damp[r], slip)

    lanes = iota((8, FZ), 1)
    group_row = jnp.concatenate(
        [
            jnp.sum(jnp.where(square, own_f[:, 12 + j : 13 + j], 0.0), axis=0, keepdims=True)
            for j in range(4)
        ],
        axis=1,
    )
    group_ids = iota((GROUPS, 4 * N), 0).astype(F32)
    group_hot = jnp.concatenate(
        [
            jnp.where(group_ids == group_row, 1.0, 0.0),
            jnp.where(group_ids == group_row + 1.0, 1.0, 0.0),
        ],
        axis=1,
    ).astype(BF16)
    here = here_f.astype(BF16)
    after = (1.0 - here.astype(F32)).astype(BF16)

    for b in range(NSB):
        wait_bytes(retm.at[span(b)], back_rs.at[b])

        @pl.loop(0, SB // UN)
        def _(q):
            for i in range(UN):
                s = b * SB + q * UN + i
                whole = retm[s].astype(F32)
                for j in range(4):
                    half, base = j // 2, 64 * (j % 2)
                    count = own_s[s, 16 + j]
                    keep = (lanes >= base) & (lanes < base + count)
                    value = jnp.where(keep, whole[:, half * FZ : (half + 1) * FZ], 0.0)
                    shift = (own_s[s, 8 + j] - base) & (FZ - 1)
                    tiles[j * N + s] = pltpu.roll(value, shift, 1)

    for r in range(0, DR, 2):
        pair = []
        for k in range(2):
            rows = tiles2(tiles, r + k)
            pair.append(jnp.concatenate([rows * here, rows * after], axis=0))
        got = dot_nn(group_hot, jnp.concatenate(pair, axis=1))
        cellv[r * GROUPS : (r + 1) * GROUPS] = got[:, 0:FZ]
        cellv[(r + 1) * GROUPS : (r + 2) * GROUPS] = got[:, FZ : 2 * FZ]
    for h in range(0, GROUPS // 2, 2):
        both = []
        for k in range(2):
            first = 2 * (h + k)
            both.append(
                jnp.concatenate(
                    [
                        cellv[pl.ds(first, 8, stride=GROUPS), :],
                        cellv[pl.ds(first + 1, 8, stride=GROUPS), :],
                    ],
                    axis=1,
                )
            )
        rbuf[h * 8 : (h + 2) * 8] = jnp.concatenate(both, axis=0).astype(BF16)

    @pl.loop(0, CHUNKS)
    def _(c):
        for i in range(PER):
            g = c * PER + i
            row = jnp.concatenate([cell[pl.ds(2 * g, 1), :], cell[pl.ds(2 * g + 1, 1), :]], axis=1)
            high = jnp.broadcast_to(row >> 8, (8, W))
            full = dot_nn(rbuf[...], lall[c, :, i * W : (i + 1) * W])
            got = jnp.zeros((8, W), F32)
            for h in range(GROUPS // 2):
                got = jnp.where(high == h, full[h * 8 : (h + 1) * 8], got)
            force_o[:, pl.ds(pl.multiple_of(g * W, W), W)] = live[pl.ds(g, 1), :] * (
                got - slip * keep8[g]
            )

    for copy in mig + halo:
        copy.wait_send()
    for b in range(NSB):
        wait_bytes(sendm.at[span(b)], am_ss.at[b])
        wait_bytes(sendr.at[span(b)], back_ss.at[b])


def per_device(
    particles, migrant_index, migrant_count, migrated_slot_cell, source_tile_size,
    tile_owner, tile_offset, closure, damping,
):
    vmem = pl.BlockSpec(memory_space=pltpu.VMEM)
    smem = pl.BlockSpec(memory_space=pltpu.SMEM)
    dma = pltpu.SemaphoreType.DMA
    scratch = [
        pltpu.VMEM((RES * CH, W), BF16),
        pltpu.VMEM((4, 2 * CH, MIG), BF16),
        pltpu.VMEM((4, 2 * CH, MIG), BF16),
        pltpu.VMEM((BLOCKS, W), F32),
        pltpu.VMEM((BLOCKS, 16, W), BF16),
        pltpu.VMEM((BLOCKS, 16, W), BF16),
        pltpu.VMEM((CHUNKS, W, KC), BF16),
        pltpu.VMEM((BLOCKS, 16, W), BF16),
        pltpu.VMEM((BLOCKS, 16, W), BF16),
        pltpu.VMEM((GROUPS // 2 * 9, KC), BF16),
        pltpu.VMEM((2, GROUPS // 2 * 9, FZ), F32),
        pltpu.VMEM((N, 8, W + EXT), BF16),
        pltpu.VMEM((N * 8, EXT), F32),
        pltpu.VMEM((N, 8, W + EXT), BF16),
        pltpu.VMEM((N, 128), I32),
        pltpu.SMEM((N, 128), I32),
        pltpu.VMEM((4 * N, 8, FZ), F32),
        pltpu.VMEM((4 * N, FZ), F32),
        pltpu.VMEM((DR * FX * FY, FZ), F32),
        pltpu.VMEM((DR * 4 * N, FZ), F32),
        pltpu.VMEM((DR * GROUPS, FZ), F32),
        pltpu.VMEM((N, 128), I32),
        pltpu.SMEM((N, 128), I32),
        pltpu.VMEM((BLOCKS, 8, W), F32),
        pltpu.VMEM((FX + 2, FY + 2, 16, FZ), F32),
        pltpu.VMEM((FX, FY * 8, FZ), F32),
        pltpu.VMEM((N, 8, W), BF16),
        pltpu.VMEM((N, 8, W), BF16),
        pltpu.VMEM((GROUPS * 4, W), BF16),
        dma((4,)), dma((4,)), dma((NSB,)), dma((NSB,)),
        dma((8,)), dma((8,)), dma((NSB,)), dma((NSB,)), dma((NSB,)), pltpu.SemaphoreType.REGULAR, dma(()),
    ]
    return pl.pallas_call(
        body,
        out_shape=(
            jax.ShapeDtypeStruct((DR, FX, FY, FZ), BF16),
            jax.ShapeDtypeStruct((DR, SLOTS), F32),
        ),
        in_specs=[vmem, vmem, smem, vmem, vmem, vmem, vmem, vmem, smem],
        out_specs=(vmem, vmem),
        scratch_shapes=scratch,
        compiler_params=pltpu.CompilerParams(
            collective_id=0, has_side_effects=True, vmem_limit_bytes=60 * 1024 * 1024
        ),
    )(
        particles,
        migrant_index,
        migrant_count,
        migrated_slot_cell.reshape(2 * BLOCKS, 128),
        source_tile_size,
        tile_owner.reshape(1, TILES),
        tile_offset.reshape(1, TILES),
        closure,
        damping,
    )


def solution(mesh):
    in_specs = (
        P(None, ("gx", "gy")),
        P(("gx", "gy"), None),
        P(("gx", "gy"), None),
        P(("gx", "gy")),
        P(("gx", "gy"), None),
        P(("gx", "gy"), None),
        P(("gx", "gy")),
        P(),
        P(),
    )
    out_specs = (P(None, "gx", "gy", None), P(None, ("gx", "gy")))
    return jax.shard_map(
        per_device, mesh=mesh, in_specs=in_specs, out_specs=out_specs, check_vma=False
    )
```

```python
import jax
import jax.numpy as jnp
from jax import lax
from jax.experimental import pallas as pl
from jax.experimental.pallas import tpu as pltpu
from jax.sharding import PartitionSpec as P

F32 = jnp.float32
BF16 = jnp.bfloat16
I32 = jnp.int32
MESH = pl.DeviceIdType.MESH

N_GX = 8
N_GY = 16
N = N_GX * N_GY
CH = 16
DR = 8
PART = 8192
MIG = 512
SLOTS = PART + 4 * MIG
TILES = 256
FX = 8
FY = 8
FZ = 128
W = 256
BLOCKS = SLOTS // W
RES = PART // W
PER = 8
CHUNKS = BLOCKS // PER
KC = PER * W
SB = 16
NSB = N // SB
GROUPS = 96
UN = 16
HOP = 21
BACK = 61
EXT = 128
SIDES = tuple((dx, dy) for dx in (-1, 0, 1) for dy in (-1, 0, 1) if dx or dy)


def dot_nn(a, b):
    return lax.dot_general(a, b, (((1,), (0,)), ((), ())), preferred_element_type=F32)


def dot_nt(a, b):
    return lax.dot_general(a, b, (((1,), (1,)), ((), ())), preferred_element_type=F32)


def iota(shape, dim):
    return lax.broadcasted_iota(I32, shape, dim)


def tiles2(tiles, r):
    return tiles.reshape(4 * N * 8, FZ)[pl.ds(r, 4 * N, stride=8), :].astype(BF16)


def wait_bytes(ref, sem):
    pltpu.make_async_copy(ref, ref, sem).wait()


def body(
    part, midx, cnt, cell, size, owner, toff, clos, damp,
    drag_o, force_o,
    pt, smig, rmig, live, rel_a, rel_b, lall, m16s, den16s, abuf, acc,
    sendm, ext, recvm, meta_v, meta_s, tiles, tden, flat, picked, cellv, own_v, own_s, keep8, gas, dtmp, sendr, retm, rbuf,
    mig_ss, mig_rs, am_ss, am_rs, halo_ss, halo_rs, back_ss, back_rs, meta_sem, rows_sem, own_sem,
):
    gx = lax.axis_index("gx")
    gy = lax.axis_index("gy")
    me = gx * N_GY + gy

    def ahead(rel):
        target = (me + rel * HOP) & (N - 1)
        return (target >> 4, target & (N_GY - 1))

    def beside(dx, dy):
        return ((gx + dx) & (N_GX - 1), (gy + dy) & (N_GY - 1))

    barrier = pltpu.get_barrier_semaphore()

    for k in range(1, N_GY):
        pl.semaphore_signal(barrier, 1, device_id=beside(0, k), device_id_type=MESH)
    for k in range(1, N_GX):
        pl.semaphore_signal(barrier, 1, device_id=beside(k, 0), device_id_type=MESH)

    @pl.loop(0, RES)
    def _(g):
        lanes = pl.ds(pl.multiple_of(g * W, W), W)
        pt[pl.ds(pl.multiple_of(g * CH, CH), CH), :] = part[:, lanes].astype(BF16)

    hits = jnp.zeros((RES, W), F32)
    for j in range(4):
        entry = midx[j : j + 1, :]
        low = entry & (W - 1)
        high = entry >> 8
        valid = iota((1, MIG), 1) < cnt[0, j]
        low_hot = jnp.where(iota((W, MIG), 0) == low, 1.0, 0.0).astype(BF16)
        found = dot_nn(pt[...], low_hot)
        state = jnp.zeros((CH, MIG), F32)
        high_b = jnp.broadcast_to(high, (CH, MIG))
        for g in range(RES):
            state = jnp.where(high_b == g, found[g * CH : (g + 1) * CH], state)
        flag = jnp.where(valid, 1.0, 0.0)
        smig[j, 0:CH] = (state * flag).astype(BF16)
        smig[j, CH : 2 * CH] = jnp.broadcast_to(flag, (CH, MIG)).astype(BF16)
        high_hot = jnp.where(iota((RES, MIG), 0) == high, flag, 0.0).astype(BF16)
        hits = hits + dot_nt(high_hot, low_hot)
    live[0:RES] = 1.0 - hits

    pl.semaphore_wait(barrier, N_GX + N_GY - 2)
    mig = []
    for j, (dx, dy) in enumerate(((1, 0), (-1, 0), (0, 1), (0, -1))):
        copy = pltpu.make_async_remote_copy(
            smig.at[j], rmig.at[j], mig_ss.at[j], mig_rs.at[j],
            device_id=beside(dx, dy), device_id_type=MESH,
        )
        copy.start()
        mig.append(copy)
    for k in range(1, N_GX):
        pl.semaphore_signal(rows_sem, 1, device_id=beside(k, 0), device_id_type=MESH)

    sub = iota((TILES, TILES), 0)
    lane = iota((TILES, TILES), 1)
    size_row = size[...].astype(F32)
    own_row = owner[...].astype(F32)
    size_col = jnp.sum(jnp.where(lane == sub, size_row, 0.0), axis=1, keepdims=True)
    start_row = jnp.sum(jnp.where(sub < lane, size_col, 0.0), axis=0, keepdims=True)
    own_col = jnp.sum(jnp.where(lane == sub, own_row, 0.0), axis=1, keepdims=True)
    earlier = jnp.where(own_col == own_row, jnp.where(sub < lane, 1.0, 0.0), 0.0)
    rank_row = jnp.sum(earlier, axis=0, keepdims=True)
    rel_row = (((owner[...] - me) * BACK) & (N - 1)).astype(F32)
    offs = toff[...]
    off_low = (offs & (FZ - 1)).astype(F32)
    off_high = (offs >> 7).astype(F32)
    sub128 = iota((N, TILES), 0)
    rank_of = (sub128 & 3).astype(F32)
    start_int = start_row.astype(I32)
    within = (start_int & 127).astype(F32)
    group = (start_int >> 7).astype(F32)
    what = jnp.where(sub128 < 4, off_low, jnp.where(sub128 < 8, off_high, 0.0))
    what = jnp.where((sub128 >= 8) & (sub128 < 12), within, what)
    what = jnp.where((sub128 >= 12) & (sub128 < 16), group, what)
    what = jnp.where((sub128 >= 16) & (sub128 < 20), size_row, what)
    what = jnp.where(rank_row == rank_of, what, 0.0).astype(BF16)
    rel_hot = jnp.where(sub128.astype(F32) == rel_row, 1.0, 0.0).astype(BF16)
    meta = dot_nt(rel_hot, what)
    own_v[...] = meta.astype(I32)
    own_copy = pltpu.make_async_copy(own_v, own_s, own_sem)
    own_copy.start()
    clos_f = clos[...]
    clos_hi = clos_f.astype(BF16)
    clos_lo = (clos_f - clos_hi.astype(F32)).astype(BF16)
    clos2 = jnp.concatenate([clos_hi.astype(F32), clos_lo.astype(F32)], axis=0).astype(BF16)

    sub16 = iota((16, W), 0)

    def prepare(g, dep, state):
        row = jnp.concatenate([cell[pl.ds(2 * g, 1), :], cell[pl.ds(2 * g + 1, 1), :]], axis=1)
        hot = jnp.where(iota((W, W), 0) == (row & (W - 1)), 1.0, 0.0).astype(BF16)
        lall[lax.div(g, PER), :, pl.ds(pl.multiple_of(lax.rem(g, PER) * W, W), W)] = hot
        near = (row >> 8) - jnp.zeros((16, W), I32)
        rel_a[g] = (near - jnp.where(sub16 >= 8, 1, 0)).astype(F32).astype(BF16)
        rel_b[g] = (near - sub16).astype(F32).astype(BF16)
        keep8[g] = state
        mixed = dot_nn(clos2, dep)
        mixed = mixed[0:8] + mixed[8:16]
        m16s[g] = jnp.concatenate([mixed, mixed], axis=0).astype(BF16)
        den16s[g] = jnp.broadcast_to(dep[0:1].astype(F32), (16, W)).astype(BF16)

    @pl.loop(0, RES)
    def _(g):
        lanes = pl.ds(pl.multiple_of(g * W, W), W)
        state = part[:, lanes]
        prepare(g, (state * live[pl.ds(g, 1), :]).astype(BF16), state[0:8])

    zero16 = jnp.zeros((16, W), BF16)

    def spread(c, first, count, row0):
        for i in range(PER):
            g = c * PER + i
            at = slice(i * W, (i + 1) * W)
            near, m16 = rel_a[g], m16s[g]
            for k in range(count // 2):
                abuf[row0 + k * 16 : row0 + (k + 1) * 16, at] = jnp.where(
                    near == float(first + 2 * k), m16, zero16
                )
            near, den = rel_b[g], den16s[g]
            for k in range(count // 16):
                abuf[row0 + count * 8 + k * 16 : row0 + count * 8 + (k + 1) * 16, at] = jnp.where(
                    near == float(first + 16 * k), den, zero16
                )

    def send_out(rel):
        sb = lax.div(rel, SB)
        pltpu.make_async_remote_copy(
            sendm.at[rel], recvm.at[rel], am_ss.at[sb], am_rs.at[sb],
            device_id=ahead(rel), device_id_type=MESH,
        ).start()

    acc[...] = jnp.zeros(acc.shape, F32)

    @pl.loop(0, RES // PER)
    def _(c):
        spread(c, 0, GROUPS // 2, 0)
        more = dot_nt(abuf[...], lall[c])
        acc[0] += more[:, 0:FZ]
        acc[1] += more[:, FZ : 2 * FZ]

    for copy in mig:
        copy.wait_recv()
    for j in range(4):
        for h in range(2):
            g = RES + 2 * j + h
            live[g : g + 1] = rmig[j, CH : 2 * CH, h * W : (h + 1) * W].astype(F32)[0:1]
            state = rmig[j, 0:CH, h * W : (h + 1) * W]
            prepare(g, state, state.astype(F32)[0:8])

    @pl.loop(RES // PER, CHUNKS)
    def _(c):
        spread(c, 0, GROUPS // 2, 0)
        more = dot_nt(abuf[...], lall[c])
        acc[0] += more[:, 0:FZ]
        acc[1] += more[:, FZ : 2 * FZ]

    own_copy.wait()
    own_f = own_v[...].astype(F32)
    begins = jnp.concatenate([own_f[:, 8 + j : 9 + j] for j in range(4)], axis=0)
    here_f = jnp.where(iota((4 * N, FZ), 1).astype(F32) >= begins, 1.0, 0.0)

    def group_cols(step):
        hots = []
        for j in range(4):
            col = own_v[:, 12 + j : 13 + j] + step
            col = (col & 1) * (GROUPS // 2) + (col >> 1)
            hots.append(jnp.where(iota((N, GROUPS), 1) == col, 1.0, 0.0))
        return jnp.concatenate(hots, axis=0)

    hot_a, hot_b = group_cols(0), group_cols(1)
    hot_a16, hot_b16 = hot_a.astype(BF16), hot_b.astype(BF16)

    def cells_of(ref_row, stride):
        return jnp.concatenate(
            [acc_at(ref_row, stride, 0), acc_at(ref_row, stride, 1)], axis=0
        )

    def acc_at(first, stride, odd):
        if stride == 1:
            return acc[odd, first : first + GROUPS // 2]
        return acc[odd, pl.ds(first, GROUPS // 2, stride=stride), :]

    for r in range(0, DR, 2):
        pair = jnp.concatenate([cells_of(r, 8), cells_of(r + 1, 8)], axis=1).astype(BF16)
        low_part, high_part = dot_nn(hot_a16, pair), dot_nn(hot_b16, pair)
        for k in range(2):
            at = slice(k * FZ, (k + 1) * FZ)
            picked[(r + k) * 4 * N : (r + k + 1) * 4 * N] = jnp.where(
                here_f > 0.0, low_part[:, at], high_part[:, at]
            )
    den = cells_of(GROUPS * 4, 1)
    den_hi = den.astype(BF16)
    den_lo = (den - den_hi.astype(F32)).astype(BF16)
    den2 = jnp.concatenate([den_hi.astype(F32), den_lo.astype(F32)], axis=1).astype(BF16)
    low_part, high_part = dot_nn(hot_a16, den2), dot_nn(hot_b16, den2)
    tden[...] = jnp.where(
        here_f > 0.0,
        low_part[:, 0:FZ] + low_part[:, FZ : 2 * FZ],
        high_part[:, 0:FZ] + high_part[:, FZ : 2 * FZ],
    )

    pl.semaphore_wait(rows_sem, N_GX - 1)
    slot_lanes = iota((8, FZ), 1)
    slot_rows = iota((8, FZ), 0)
    @pl.loop(0, NSB)
    def _(b):
        for _i in range(1):
            for i in range(SB):
                s = b * SB + i
                halves, dens = [], []
                for half in range(2):
                    total = jnp.zeros((8, FZ), F32)
                    dtotal = jnp.zeros((8, FZ), F32)
                    for j in (2 * half, 2 * half + 1):
                        base = 64 * (j % 2)
                        count = own_s[s, 16 + j]
                        shift = (base - own_s[s, 8 + j]) & (FZ - 1)
                        keep = (slot_lanes >= base) & (slot_lanes < base + count)
                        value = picked[pl.ds(j * N + s, 8, stride=4 * N), :]
                        total = jnp.where(keep, pltpu.roll(value, shift, 1), total)
                        dval = jnp.broadcast_to(tden[pl.ds(j * N + s, 1), :], (8, FZ))
                        dtotal = jnp.where(keep, pltpu.roll(dval, shift, 1), dtotal)
                    halves.append(total)
                    dens.append(dtotal)
                sendm[s, :, 0:W] = jnp.concatenate(halves, axis=1).astype(BF16)
                value = jnp.where((slot_rows & 1) == 0, dens[0], dens[1])
                top = value.astype(BF16).astype(F32)
                note = jnp.broadcast_to(own_v[pl.ds(s, 1), :].astype(F32), (8, FZ))
                extra = jnp.where(
                    slot_rows < 2, top, jnp.where(slot_rows < 4, value - top, note)
                )
                sendm[s, :, W : W + EXT] = extra.astype(BF16)

        @pl.when(b == 0)
        def _():
            recvm[0] = sendm[0]

        @pl.loop(0, SB)
        def _(k):
            pl.when(b * SB + k > 0)(lambda: send_out(b * SB + k))

    def span(b):
        return pl.ds(1, SB - 1) if b == 0 else pl.ds(b * SB, SB)

    lane_row = iota((1, FZ), 1)
    first_half = lane_row < 64

    def place(b):
        wait_bytes(meta_s.at[pl.ds(b * SB, SB)], meta_sem.at[b])

        @pl.loop(0, SB // UN)
        def _(q):
            for i in range(UN):
                s = b * SB + q * UN + i
                whole = recvm[s, :, 0:W].astype(F32)
                for j in range(4):
                    half = j // 2
                    keep = first_half if j % 2 == 0 else ~first_half
                    shift = (meta_s[s, j] + (0 if j % 2 == 0 else 64)) & (FZ - 1)
                    at = slice(half * FZ, (half + 1) * FZ)
                    tiles[j * N + s] = pltpu.roll(jnp.where(keep, whole[:, at], 0.0), shift, 1)
                    den = ext[pl.ds(s * 8 + half, 1), :] + ext[pl.ds(s * 8 + 2 + half, 1), :]
                    den = jnp.broadcast_to(jnp.where(keep, den, 0.0), (8, FZ))
                    tden[pl.ds(j * N + s, 1), :] = pltpu.roll(den, shift, 1)[0:1]

    for b in range(NSB):
        wait_bytes(recvm.at[span(b)], am_rs.at[b])
        ext[b * SB * 8 : (b + 1) * SB * 8] = (
            recvm[b * SB : (b + 1) * SB, :, W : W + EXT].astype(F32).reshape(SB * 8, EXT)
        )
        meta_v[b * SB : (b + 1) * SB] = ext[pl.ds(b * SB * 8 + 4, SB, stride=8), :].astype(I32)
        pltpu.make_async_copy(
            meta_v.at[pl.ds(b * SB, SB)], meta_s.at[pl.ds(b * SB, SB)], meta_sem.at[b]
        ).start()

        if b > 0:
            place(b - 1)
    place(NSB - 1)

    square = iota((N, N), 0) == iota((N, N), 1)
    meta_f = meta_v[...].astype(F32)
    cols = []
    for j in range(4):
        cols.append(
            jnp.sum(jnp.where(square, meta_f[:, 4 + j : 5 + j], 0.0), axis=0, keepdims=True)
        )
    col_row = jnp.concatenate(cols, axis=1)
    col_hot = jnp.where(iota((FX * FY, 4 * N), 0).astype(F32) == col_row, 1.0, 0.0)
    for r in range(0, DR, 2):
        pair = [tiles2(tiles, r), tiles2(tiles, r + 1)]
        sums = dot_nn(col_hot.astype(BF16), jnp.concatenate(pair, axis=1))
        flat[r * 64 : (r + 1) * 64] = sums[:, 0:FZ]
        flat[(r + 1) * 64 : (r + 2) * 64] = sums[:, FZ : 2 * FZ]
    den = lax.dot_general(
        col_hot, tden[...], (((1,), (0,)), ((), ())),
        precision=lax.Precision.HIGHEST, preferred_element_type=F32,
    )
    for x in range(FX):
        for y in range(FY):
            c = x * FY + y
            gas[x + 1, y + 1, 0:8] = flat[pl.ds(c, 8, stride=64), :]
            gas[x + 1, y + 1, 8:16] = jnp.broadcast_to(den[c : c + 1], (8, FZ))

    def edge(step, far):
        if step == 0:
            return pl.ds(1, 8)
        if far:
            return pl.ds(0 if step > 0 else 9, 1)
        return pl.ds(8 if step > 0 else 1, 1)

    halo = []
    for i, (dx, dy) in enumerate(SIDES):
        copy = pltpu.make_async_remote_copy(
            gas.at[edge(dx, False), edge(dy, False)], gas.at[edge(dx, True), edge(dy, True)],
            halo_ss.at[i], halo_rs.at[i], device_id=beside(dx, dy), device_id_type=MESH,
        )
        copy.start()
        halo.append(copy)
    for copy in halo:
        copy.wait_recv()

    @pl.loop(0, FX // 2)
    def _(x2):
        for odd in range(2):
            x = 2 * x2 + odd
            over_x = [gas[x, y] + 2.0 * gas[x + 1, y] + gas[x + 2, y] for y in range(FY + 2)]
            for y in range(FY):
                smooth = (over_x[y] + 2.0 * over_x[y + 1] + over_x[y + 2]) * (1.0 / 16.0)
                dens = smooth[8:16]
                drag = smooth[0:8] / (1.0 + dens * dens)
                dtmp[x, y * 8 : (y + 1) * 8] = drag

    tile_hot = jnp.concatenate(
        [
            jnp.where(iota((N, FX * FY), 1).astype(F32) == meta_f[:, 4 + j : 5 + j], 1.0, 0.0)
            for j in range(4)
        ],
        axis=0,
    ).astype(BF16)
    drag_rows = dtmp.reshape(FX * FY * 8, FZ)
    for r in range(0, DR, 2):
        pair = [drag_rows[pl.ds(r + k, FX * FY, stride=8), :].astype(BF16) for k in range(2)]
        got = dot_nn(tile_hot, jnp.concatenate(pair, axis=1))
        picked[r * 4 * N : (r + 1) * 4 * N] = got[:, 0:FZ]
        picked[(r + 1) * 4 * N : (r + 2) * 4 * N] = got[:, FZ : 2 * FZ]

    for b in range(NSB):
        @pl.loop(0, SB // UN)
        def _(q):
            for i in range(UN):
                s = b * SB + q * UN + i
                halves = []
                for half in range(2):
                    pair = []
                    for j in (2 * half, 2 * half + 1):
                        shift = ((0 if j % 2 == 0 else 64) - meta_s[s, j]) & (FZ - 1)
                        pair.append(
                            pltpu.roll(picked[pl.ds(j * N + s, 8, stride=4 * N), :], shift, 1)
                        )
                    halves.append(jnp.where(first_half, pair[0], pair[1]))
                sendr[s] = jnp.concatenate(halves, axis=1).astype(BF16)

        if b == 0:
            retm[0] = sendr[0]

        @pl.loop(1 if b == 0 else b * SB, (b + 1) * SB)
        def _(rel):
            pltpu.make_async_remote_copy(
                sendr.at[rel], retm.at[rel], back_ss.at[b], back_rs.at[b],
                device_id=ahead(N - rel), device_id_type=MESH,
            ).start()

    for r in range(DR):
        for x in range(FX):
            drag_o[r, x] = dtmp[x, pl.ds(r, FY, stride=8), :].astype(BF16)

    rows8 = iota((8, W), 0)
    slip = jnp.zeros((8, W), F32)
    for r in range(DR):
        slip = jnp.where(rows8 == r, damp[r], slip)

    lanes = iota((8, FZ), 1)
    group_row = jnp.concatenate(
        [
            jnp.sum(jnp.where(square, own_f[:, 12 + j : 13 + j], 0.0), axis=0, keepdims=True)
            for j in range(4)
        ],
        axis=1,
    )
    group_ids = iota((GROUPS, 4 * N), 0).astype(F32)
    group_hot = jnp.concatenate(
        [
            jnp.where(group_ids == group_row, 1.0, 0.0),
            jnp.where(group_ids == group_row + 1.0, 1.0, 0.0),
        ],
        axis=1,
    ).astype(BF16)
    here = here_f.astype(BF16)
    after = (1.0 - here.astype(F32)).astype(BF16)

    for b in range(NSB):
        wait_bytes(retm.at[span(b)], back_rs.at[b])

        @pl.loop(0, SB // UN)
        def _(q):
            for i in range(UN):
                s = b * SB + q * UN + i
                whole = retm[s].astype(F32)
                for j in range(4):
                    half, base = j // 2, 64 * (j % 2)
                    count = own_s[s, 16 + j]
                    keep = (lanes >= base) & (lanes < base + count)
                    value = jnp.where(keep, whole[:, half * FZ : (half + 1) * FZ], 0.0)
                    shift = (own_s[s, 8 + j] - base) & (FZ - 1)
                    tiles[j * N + s] = pltpu.roll(value, shift, 1)

    for r in range(0, DR, 2):
        pair = []
        for k in range(2):
            rows = tiles2(tiles, r + k)
            pair.append(jnp.concatenate([rows * here, rows * after], axis=0))
        got = dot_nn(group_hot, jnp.concatenate(pair, axis=1))
        cellv[r * GROUPS : (r + 1) * GROUPS] = got[:, 0:FZ]
        cellv[(r + 1) * GROUPS : (r + 2) * GROUPS] = got[:, FZ : 2 * FZ]
    for h in range(0, GROUPS // 2, 2):
        both = []
        for k in range(2):
            first = 2 * (h + k)
            both.append(
                jnp.concatenate(
                    [
                        cellv[pl.ds(first, 8, stride=GROUPS), :],
                        cellv[pl.ds(first + 1, 8, stride=GROUPS), :],
                    ],
                    axis=1,
                )
            )
        rbuf[h * 8 : (h + 2) * 8] = jnp.concatenate(both, axis=0).astype(BF16)

    @pl.loop(0, CHUNKS)
    def _(c):
        for i in range(PER):
            g = c * PER + i
            row = jnp.concatenate([cell[pl.ds(2 * g, 1), :], cell[pl.ds(2 * g + 1, 1), :]], axis=1)
            high = jnp.broadcast_to(row >> 8, (8, W))
            full = dot_nn(rbuf[...], lall[c, :, i * W : (i + 1) * W])
            got = jnp.zeros((8, W), F32)
            for h in range(GROUPS // 2):
                got = jnp.where(high == h, full[h * 8 : (h + 1) * 8], got)
            force_o[:, pl.ds(pl.multiple_of(g * W, W), W)] = live[pl.ds(g, 1), :] * (
                got - slip * keep8[g]
            )

    for copy in mig + halo:
        copy.wait_send()
    for b in range(NSB):
        wait_bytes(sendm.at[span(b)], am_ss.at[b])
        wait_bytes(sendr.at[span(b)], back_ss.at[b])


def per_device(
    particles, migrant_index, migrant_count, migrated_slot_cell, source_tile_size,
    tile_owner, tile_offset, closure, damping,
):
    vmem = pl.BlockSpec(memory_space=pltpu.VMEM)
    smem = pl.BlockSpec(memory_space=pltpu.SMEM)
    dma = pltpu.SemaphoreType.DMA
    scratch = [
        pltpu.VMEM((RES * CH, W), BF16),
        pltpu.VMEM((4, 2 * CH, MIG), BF16),
        pltpu.VMEM((4, 2 * CH, MIG), BF16),
        pltpu.VMEM((BLOCKS, W), F32),
        pltpu.VMEM((BLOCKS, 16, W), BF16),
        pltpu.VMEM((BLOCKS, 16, W), BF16),
        pltpu.VMEM((CHUNKS, W, KC), BF16),
        pltpu.VMEM((BLOCKS, 16, W), BF16),
        pltpu.VMEM((BLOCKS, 16, W), BF16),
        pltpu.VMEM((GROUPS // 2 * 9, KC), BF16),
        pltpu.VMEM((2, GROUPS // 2 * 9, FZ), F32),
        pltpu.VMEM((N, 8, W + EXT), BF16),
        pltpu.VMEM((N * 8, EXT), F32),
        pltpu.VMEM((N, 8, W + EXT), BF16),
        pltpu.VMEM((N, 128), I32),
        pltpu.SMEM((N, 128), I32),
        pltpu.VMEM((4 * N, 8, FZ), F32),
        pltpu.VMEM((4 * N, FZ), F32),
        pltpu.VMEM((DR * FX * FY, FZ), F32),
        pltpu.VMEM((DR * 4 * N, FZ), F32),
        pltpu.VMEM((DR * GROUPS, FZ), F32),
        pltpu.VMEM((N, 128), I32),
        pltpu.SMEM((N, 128), I32),
        pltpu.VMEM((BLOCKS, 8, W), F32),
        pltpu.VMEM((FX + 2, FY + 2, 16, FZ), F32),
        pltpu.VMEM((FX, FY * 8, FZ), F32),
        pltpu.VMEM((N, 8, W), BF16),
        pltpu.VMEM((N, 8, W), BF16),
        pltpu.VMEM((GROUPS * 4, W), BF16),
        dma((4,)), dma((4,)), dma((NSB,)), dma((NSB,)),
        dma((8,)), dma((8,)), dma((NSB,)), dma((NSB,)), dma((NSB,)), pltpu.SemaphoreType.REGULAR, dma(()),
    ]
    return pl.pallas_call(
        body,
        out_shape=(
            jax.ShapeDtypeStruct((DR, FX, FY, FZ), BF16),
            jax.ShapeDtypeStruct((DR, SLOTS), F32),
        ),
        in_specs=[vmem, vmem, smem, vmem, vmem, vmem, vmem, vmem, smem],
        out_specs=(vmem, vmem),
        scratch_shapes=scratch,
        compiler_params=pltpu.CompilerParams(
            collective_id=0, has_side_effects=True, vmem_limit_bytes=60 * 1024 * 1024
        ),
    )(
        particles,
        migrant_index,
        migrant_count,
        migrated_slot_cell.reshape(2 * BLOCKS, 128),
        source_tile_size,
        tile_owner.reshape(1, TILES),
        tile_offset.reshape(1, TILES),
        closure,
        damping,
    )


def solution(mesh):
    in_specs = (
        P(None, ("gx", "gy")),
        P(("gx", "gy"), None),
        P(("gx", "gy"), None),
        P(("gx", "gy")),
        P(("gx", "gy"), None),
        P(("gx", "gy"), None),
        P(("gx", "gy")),
        P(),
        P(),
    )
    out_specs = (P(None, "gx", "gy", None), P(None, ("gx", "gy")))
    return jax.shard_map(
        per_device, mesh=mesh, in_specs=in_specs, out_specs=out_specs, check_vma=False
    )
```

```python
import jax
import jax.numpy as jnp
from jax import lax
from jax.experimental import pallas as pl
from jax.experimental.pallas import tpu as pltpu
from jax.sharding import PartitionSpec as P

F32 = jnp.float32
BF16 = jnp.bfloat16
I32 = jnp.int32
MESH = pl.DeviceIdType.MESH

N_GX = 8
N_GY = 16
N = N_GX * N_GY
CH = 16
DR = 8
PART = 8192
MIG = 512
SLOTS = PART + 4 * MIG
TILES = 256
FX = 8
FY = 8
FZ = 128
W = 256
BLOCKS = SLOTS // W
RES = PART // W
PER = 8
CHUNKS = BLOCKS // PER
KC = PER * W
SB = 16
NSB = N // SB
GROUPS = 96
UN = 16
HOP = 21
BACK = 61
EXT = 128
SIDES = tuple((dx, dy) for dx in (-1, 0, 1) for dy in (-1, 0, 1) if dx or dy)


def dot_nn(a, b):
    return lax.dot_general(a, b, (((1,), (0,)), ((), ())), preferred_element_type=F32)


def dot_nt(a, b):
    return lax.dot_general(a, b, (((1,), (1,)), ((), ())), preferred_element_type=F32)


def iota(shape, dim):
    return lax.broadcasted_iota(I32, shape, dim)


def tiles2(tiles, r):
    return tiles.reshape(4 * N * 8, FZ)[pl.ds(r, 4 * N, stride=8), :].astype(BF16)


def wait_bytes(ref, sem):
    pltpu.make_async_copy(ref, ref, sem).wait()


def body(
    part, midx, cnt, cell, size, owner, toff, clos, damp,
    drag_o, force_o,
    pt, smig, rmig, live, rel_a, rel_b, lall, m16s, den16s, abuf, acc,
    sendm, ext, recvm, meta_v, meta_s, tiles, tden, flat, picked, cellv, own_v, own_s, keep8, gas, gden, dtmp, sendr, retm, rbuf,
    mig_ss, mig_rs, am_ss, am_rs, halo_ss, halo_rs, back_ss, back_rs, meta_sem, rows_sem, own_sem,
):
    gx = lax.axis_index("gx")
    gy = lax.axis_index("gy")
    me = gx * N_GY + gy

    def ahead(rel):
        target = (me + rel * HOP) & (N - 1)
        return (target >> 4, target & (N_GY - 1))

    def beside(dx, dy):
        return ((gx + dx) & (N_GX - 1), (gy + dy) & (N_GY - 1))

    barrier = pltpu.get_barrier_semaphore()

    for k in range(1, N_GY):
        pl.semaphore_signal(barrier, 1, device_id=beside(0, k), device_id_type=MESH)
    for k in range(1, N_GX):
        pl.semaphore_signal(barrier, 1, device_id=beside(k, 0), device_id_type=MESH)

    @pl.loop(0, RES)
    def _(g):
        lanes = pl.ds(pl.multiple_of(g * W, W), W)
        pt[pl.ds(pl.multiple_of(g * CH, CH), CH), :] = part[:, lanes].astype(BF16)

    hits = jnp.zeros((RES, W), F32)
    for j in range(4):
        entry = midx[j : j + 1, :]
        low = entry & (W - 1)
        high = entry >> 8
        valid = iota((1, MIG), 1) < cnt[0, j]
        low_hot = jnp.where(iota((W, MIG), 0) == low, 1.0, 0.0).astype(BF16)
        found = dot_nn(pt[...], low_hot)
        state = jnp.zeros((CH, MIG), F32)
        high_b = jnp.broadcast_to(high, (CH, MIG))
        for g in range(RES):
            state = jnp.where(high_b == g, found[g * CH : (g + 1) * CH], state)
        flag = jnp.where(valid, 1.0, 0.0)
        smig[j, 0:CH] = (state * flag).astype(BF16)
        smig[j, CH : 2 * CH] = jnp.broadcast_to(flag, (CH, MIG)).astype(BF16)
        high_hot = jnp.where(iota((RES, MIG), 0) == high, flag, 0.0).astype(BF16)
        hits = hits + dot_nt(high_hot, low_hot)
    live[0:RES] = 1.0 - hits

    pl.semaphore_wait(barrier, N_GX + N_GY - 2)
    mig = []
    for j, (dx, dy) in enumerate(((1, 0), (-1, 0), (0, 1), (0, -1))):
        copy = pltpu.make_async_remote_copy(
            smig.at[j], rmig.at[j], mig_ss.at[j], mig_rs.at[j],
            device_id=beside(dx, dy), device_id_type=MESH,
        )
        copy.start()
        mig.append(copy)
    for k in range(1, N_GX):
        pl.semaphore_signal(rows_sem, 1, device_id=beside(k, 0), device_id_type=MESH)

    sub = iota((TILES, TILES), 0)
    lane = iota((TILES, TILES), 1)
    size_row = size[...].astype(F32)
    own_row = owner[...].astype(F32)
    size_col = jnp.sum(jnp.where(lane == sub, size_row, 0.0), axis=1, keepdims=True)
    start_row = jnp.sum(jnp.where(sub < lane, size_col, 0.0), axis=0, keepdims=True)
    own_col = jnp.sum(jnp.where(lane == sub, own_row, 0.0), axis=1, keepdims=True)
    earlier = jnp.where(own_col == own_row, jnp.where(sub < lane, 1.0, 0.0), 0.0)
    rank_row = jnp.sum(earlier, axis=0, keepdims=True)
    rel_row = (((owner[...] - me) * BACK) & (N - 1)).astype(F32)
    offs = toff[...]
    off_low = (offs & (FZ - 1)).astype(F32)
    off_high = (offs >> 7).astype(F32)
    sub128 = iota((N, TILES), 0)
    rank_of = (sub128 & 3).astype(F32)
    start_int = start_row.astype(I32)
    within = (start_int & 127).astype(F32)
    group = (start_int >> 7).astype(F32)
    what = jnp.where(sub128 < 4, off_low, jnp.where(sub128 < 8, off_high, 0.0))
    what = jnp.where((sub128 >= 8) & (sub128 < 12), within, what)
    what = jnp.where((sub128 >= 12) & (sub128 < 16), group, what)
    what = jnp.where((sub128 >= 16) & (sub128 < 20), size_row, what)
    what = jnp.where(rank_row == rank_of, what, 0.0).astype(BF16)
    rel_hot = jnp.where(sub128.astype(F32) == rel_row, 1.0, 0.0).astype(BF16)
    meta = dot_nt(rel_hot, what)
    own_v[...] = meta.astype(I32)
    own_copy = pltpu.make_async_copy(own_v, own_s, own_sem)
    own_copy.start()
    clos_f = clos[...]
    clos_hi = clos_f.astype(BF16)
    clos_lo = (clos_f - clos_hi.astype(F32)).astype(BF16)
    clos2 = jnp.concatenate([clos_hi.astype(F32), clos_lo.astype(F32)], axis=0).astype(BF16)

    sub16 = iota((16, W), 0)

    def prepare(g, dep, state):
        row = jnp.concatenate([cell[pl.ds(2 * g, 1), :], cell[pl.ds(2 * g + 1, 1), :]], axis=1)
        hot = jnp.where(iota((W, W), 0) == (row & (W - 1)), 1.0, 0.0).astype(BF16)
        lall[lax.div(g, PER), :, pl.ds(pl.multiple_of(lax.rem(g, PER) * W, W), W)] = hot
        near = (row >> 8) - jnp.zeros((16, W), I32)
        rel_a[g] = (near - jnp.where(sub16 >= 8, 1, 0)).astype(F32).astype(BF16)
        rel_b[g] = (near - sub16).astype(F32).astype(BF16)
        keep8[g] = state
        mixed = dot_nn(clos2, dep)
        mixed = mixed[0:8] + mixed[8:16]
        m16s[g] = jnp.concatenate([mixed, mixed], axis=0).astype(BF16)
        den16s[g] = jnp.broadcast_to(dep[0:1].astype(F32), (16, W)).astype(BF16)

    @pl.loop(0, RES)
    def _(g):
        lanes = pl.ds(pl.multiple_of(g * W, W), W)
        state = part[:, lanes]
        prepare(g, (state * live[pl.ds(g, 1), :]).astype(BF16), state[0:8])

    zero16 = jnp.zeros((16, W), BF16)

    def spread(c, first, count, row0):
        for i in range(PER):
            g = c * PER + i
            at = slice(i * W, (i + 1) * W)
            near, m16 = rel_a[g], m16s[g]
            for k in range(count // 2):
                abuf[row0 + k * 16 : row0 + (k + 1) * 16, at] = jnp.where(
                    near == float(first + 2 * k), m16, zero16
                )
            near, den = rel_b[g], den16s[g]
            for k in range(count // 16):
                abuf[row0 + count * 8 + k * 16 : row0 + count * 8 + (k + 1) * 16, at] = jnp.where(
                    near == float(first + 16 * k), den, zero16
                )

    def send_out(rel):
        sb = lax.div(rel, SB)
        pltpu.make_async_remote_copy(
            sendm.at[rel], recvm.at[rel], am_ss.at[sb], am_rs.at[sb],
            device_id=ahead(rel), device_id_type=MESH,
        ).start()

    acc[...] = jnp.zeros(acc.shape, F32)

    @pl.loop(0, RES // PER)
    def _(c):
        spread(c, 0, GROUPS // 2, 0)
        more = dot_nt(abuf[...], lall[c])
        acc[0] += more[:, 0:FZ]
        acc[1] += more[:, FZ : 2 * FZ]

    for copy in mig:
        copy.wait_recv()
    for j in range(4):
        for h in range(2):
            g = RES + 2 * j + h
            live[g : g + 1] = rmig[j, CH : 2 * CH, h * W : (h + 1) * W].astype(F32)[0:1]
            state = rmig[j, 0:CH, h * W : (h + 1) * W]
            prepare(g, state, state.astype(F32)[0:8])

    @pl.loop(RES // PER, CHUNKS)
    def _(c):
        spread(c, 0, GROUPS // 2, 0)
        more = dot_nt(abuf[...], lall[c])
        acc[0] += more[:, 0:FZ]
        acc[1] += more[:, FZ : 2 * FZ]

    own_copy.wait()
    own_f = own_v[...].astype(F32)
    begins = jnp.concatenate([own_f[:, 8 + j : 9 + j] for j in range(4)], axis=0)
    here_f = jnp.where(iota((4 * N, FZ), 1).astype(F32) >= begins, 1.0, 0.0)

    def group_cols(step):
        hots = []
        for j in range(4):
            col = own_v[:, 12 + j : 13 + j] + step
            col = (col & 1) * (GROUPS // 2) + (col >> 1)
            hots.append(jnp.where(iota((N, GROUPS), 1) == col, 1.0, 0.0))
        return jnp.concatenate(hots, axis=0)

    hot_a, hot_b = group_cols(0), group_cols(1)
    hot_a16, hot_b16 = hot_a.astype(BF16), hot_b.astype(BF16)

    def cells_of(ref_row, stride):
        return jnp.concatenate(
            [acc_at(ref_row, stride, 0), acc_at(ref_row, stride, 1)], axis=0
        )

    def acc_at(first, stride, odd):
        if stride == 1:
            return acc[odd, first : first + GROUPS // 2]
        return acc[odd, pl.ds(first, GROUPS // 2, stride=stride), :]

    for r in range(0, DR, 2):
        pair = jnp.concatenate([cells_of(r, 8), cells_of(r + 1, 8)], axis=1).astype(BF16)
        low_part, high_part = dot_nn(hot_a16, pair), dot_nn(hot_b16, pair)
        for k in range(2):
            at = slice(k * FZ, (k + 1) * FZ)
            picked[(r + k) * 4 * N : (r + k + 1) * 4 * N] = jnp.where(
                here_f > 0.0, low_part[:, at], high_part[:, at]
            )
    den = cells_of(GROUPS * 4, 1)
    den_hi = den.astype(BF16)
    den_lo = (den - den_hi.astype(F32)).astype(BF16)
    den2 = jnp.concatenate([den_hi.astype(F32), den_lo.astype(F32)], axis=1).astype(BF16)
    low_part, high_part = dot_nn(hot_a16, den2), dot_nn(hot_b16, den2)
    tden[...] = jnp.where(
        here_f > 0.0,
        low_part[:, 0:FZ] + low_part[:, FZ : 2 * FZ],
        high_part[:, 0:FZ] + high_part[:, FZ : 2 * FZ],
    )

    pl.semaphore_wait(rows_sem, N_GX - 1)
    slot_lanes = iota((8, FZ), 1)
    slot_rows = iota((8, FZ), 0)
    @pl.loop(0, NSB)
    def _(b):
        for _i in range(1):
            for i in range(SB):
                s = b * SB + i
                halves, dens = [], []
                for half in range(2):
                    total = jnp.zeros((8, FZ), F32)
                    dtotal = jnp.zeros((8, FZ), F32)
                    for j in (2 * half, 2 * half + 1):
                        base = 64 * (j % 2)
                        count = own_s[s, 16 + j]
                        shift = (base - own_s[s, 8 + j]) & (FZ - 1)
                        keep = (slot_lanes >= base) & (slot_lanes < base + count)
                        value = picked[pl.ds(j * N + s, 8, stride=4 * N), :]
                        total = jnp.where(keep, pltpu.roll(value, shift, 1), total)
                        dval = jnp.broadcast_to(tden[pl.ds(j * N + s, 1), :], (8, FZ))
                        dtotal = jnp.where(keep, pltpu.roll(dval, shift, 1), dtotal)
                    halves.append(total)
                    dens.append(dtotal)
                sendm[s, :, 0:W] = jnp.concatenate(halves, axis=1).astype(BF16)
                value = jnp.where((slot_rows & 1) == 0, dens[0], dens[1])
                top = value.astype(BF16).astype(F32)
                note = jnp.broadcast_to(own_v[pl.ds(s, 1), :].astype(F32), (8, FZ))
                extra = jnp.where(
                    slot_rows < 2, top, jnp.where(slot_rows < 4, value - top, note)
                )
                sendm[s, :, W : W + EXT] = extra.astype(BF16)

        @pl.when(b == 0)
        def _():
            recvm[0] = sendm[0]

        @pl.loop(0, SB)
        def _(k):
            pl.when(b * SB + k > 0)(lambda: send_out(b * SB + k))

    def span(b):
        return pl.ds(1, SB - 1) if b == 0 else pl.ds(b * SB, SB)

    lane_row = iota((1, FZ), 1)
    first_half = lane_row < 64

    def place(b):
        wait_bytes(meta_s.at[pl.ds(b * SB, SB)], meta_sem.at[b])

        @pl.loop(0, SB // UN)
        def _(q):
            for i in range(UN):
                s = b * SB + q * UN + i
                whole = recvm[s, :, 0:W].astype(F32)
                for j in range(4):
                    half = j // 2
                    keep = first_half if j % 2 == 0 else ~first_half
                    shift = (meta_s[s, j] + (0 if j % 2 == 0 else 64)) & (FZ - 1)
                    at = slice(half * FZ, (half + 1) * FZ)
                    tiles[j * N + s] = pltpu.roll(jnp.where(keep, whole[:, at], 0.0), shift, 1)
                    den = ext[pl.ds(s * 8 + half, 1), :] + ext[pl.ds(s * 8 + 2 + half, 1), :]
                    den = jnp.broadcast_to(jnp.where(keep, den, 0.0), (8, FZ))
                    tden[pl.ds(j * N + s, 1), :] = pltpu.roll(den, shift, 1)[0:1]

    for b in range(NSB):
        wait_bytes(recvm.at[span(b)], am_rs.at[b])
        ext[b * SB * 8 : (b + 1) * SB * 8] = (
            recvm[b * SB : (b + 1) * SB, :, W : W + EXT].astype(F32).reshape(SB * 8, EXT)
        )
        meta_v[b * SB : (b + 1) * SB] = ext[pl.ds(b * SB * 8 + 4, SB, stride=8), :].astype(I32)
        pltpu.make_async_copy(
            meta_v.at[pl.ds(b * SB, SB)], meta_s.at[pl.ds(b * SB, SB)], meta_sem.at[b]
        ).start()

        if b > 0:
            place(b - 1)
    place(NSB - 1)

    square = iota((N, N), 0) == iota((N, N), 1)
    meta_f = meta_v[...].astype(F32)
    cols = []
    for j in range(4):
        cols.append(
            jnp.sum(jnp.where(square, meta_f[:, 4 + j : 5 + j], 0.0), axis=0, keepdims=True)
        )
    col_row = jnp.concatenate(cols, axis=1)
    col_hot = jnp.where(iota((FX * FY, 4 * N), 0).astype(F32) == col_row, 1.0, 0.0)
    for r in range(0, DR, 2):
        pair = [tiles2(tiles, r), tiles2(tiles, r + 1)]
        sums = dot_nn(col_hot.astype(BF16), jnp.concatenate(pair, axis=1))
        flat[r * 64 : (r + 1) * 64] = sums[:, 0:FZ]
        flat[(r + 1) * 64 : (r + 2) * 64] = sums[:, FZ : 2 * FZ]
    den = lax.dot_general(
        col_hot, tden[...], (((1,), (0,)), ((), ())),
        precision=lax.Precision.HIGHEST, preferred_element_type=F32,
    )
    for x in range(FX):
        for y in range(FY):
            c = x * FY + y
            gas[x + 1, y + 1] = flat[pl.ds(c, 8, stride=64), :]
            gden[x + 1, y + 1] = den[c : c + 1]

    def edge(step, far):
        if step == 0:
            return pl.ds(1, 8)
        if far:
            return pl.ds(0 if step > 0 else 9, 1)
        return pl.ds(8 if step > 0 else 1, 1)

    halo = []
    for i, (dx, dy) in enumerate(SIDES):
        for k, block in enumerate((gas, gden)):
            copy = pltpu.make_async_remote_copy(
                block.at[edge(dx, False), edge(dy, False)],
                block.at[edge(dx, True), edge(dy, True)],
                halo_ss.at[2 * i + k], halo_rs.at[2 * i + k],
                device_id=beside(dx, dy), device_id_type=MESH,
            )
            copy.start()
            halo.append(copy)
    for copy in halo:
        copy.wait_recv()

    @pl.loop(0, FX // 2)
    def _(x2):
        for odd in range(2):
            x = 2 * x2 + odd
            over_x = [gas[x, y] + 2.0 * gas[x + 1, y] + gas[x + 2, y] for y in range(FY + 2)]
            den_x = [gden[x, y] + 2.0 * gden[x + 1, y] + gden[x + 2, y] for y in range(FY + 2)]
            for y in range(FY):
                smooth = (over_x[y] + 2.0 * over_x[y + 1] + over_x[y + 2]) * (1.0 / 16.0)
                dens = (den_x[y] + 2.0 * den_x[y + 1] + den_x[y + 2]) * (1.0 / 16.0)
                drag = smooth / (1.0 + dens * dens)
                dtmp[x, y * 8 : (y + 1) * 8] = drag

    tile_hot = jnp.concatenate(
        [
            jnp.where(iota((N, FX * FY), 1).astype(F32) == meta_f[:, 4 + j : 5 + j], 1.0, 0.0)
            for j in range(4)
        ],
        axis=0,
    ).astype(BF16)
    drag_rows = dtmp.reshape(FX * FY * 8, FZ)
    for r in range(0, DR, 2):
        pair = [drag_rows[pl.ds(r + k, FX * FY, stride=8), :].astype(BF16) for k in range(2)]
        got = dot_nn(tile_hot, jnp.concatenate(pair, axis=1))
        picked[r * 4 * N : (r + 1) * 4 * N] = got[:, 0:FZ]
        picked[(r + 1) * 4 * N : (r + 2) * 4 * N] = got[:, FZ : 2 * FZ]

    for b in range(NSB):
        @pl.loop(0, SB // UN)
        def _(q):
            for i in range(UN):
                s = b * SB + q * UN + i
                halves = []
                for half in range(2):
                    pair = []
                    for j in (2 * half, 2 * half + 1):
                        shift = ((0 if j % 2 == 0 else 64) - meta_s[s, j]) & (FZ - 1)
                        pair.append(
                            pltpu.roll(picked[pl.ds(j * N + s, 8, stride=4 * N), :], shift, 1)
                        )
                    halves.append(jnp.where(first_half, pair[0], pair[1]))
                sendr[s] = jnp.concatenate(halves, axis=1).astype(BF16)

        if b == 0:
            retm[0] = sendr[0]

        @pl.loop(1 if b == 0 else b * SB, (b + 1) * SB)
        def _(rel):
            pltpu.make_async_remote_copy(
                sendr.at[rel], retm.at[rel], back_ss.at[b], back_rs.at[b],
                device_id=ahead(N - rel), device_id_type=MESH,
            ).start()

    for r in range(DR):
        for x in range(FX):
            drag_o[r, x] = dtmp[x, pl.ds(r, FY, stride=8), :].astype(BF16)

    rows8 = iota((8, W), 0)
    slip = jnp.zeros((8, W), F32)
    for r in range(DR):
        slip = jnp.where(rows8 == r, damp[r], slip)

    lanes = iota((8, FZ), 1)
    group_row = jnp.concatenate(
        [
            jnp.sum(jnp.where(square, own_f[:, 12 + j : 13 + j], 0.0), axis=0, keepdims=True)
            for j in range(4)
        ],
        axis=1,
    )
    group_ids = iota((GROUPS, 4 * N), 0).astype(F32)
    group_hot = jnp.concatenate(
        [
            jnp.where(group_ids == group_row, 1.0, 0.0),
            jnp.where(group_ids == group_row + 1.0, 1.0, 0.0),
        ],
        axis=1,
    ).astype(BF16)
    here = here_f.astype(BF16)
    after = (1.0 - here.astype(F32)).astype(BF16)

    for b in range(NSB):
        wait_bytes(retm.at[span(b)], back_rs.at[b])

        @pl.loop(0, SB // UN)
        def _(q):
            for i in range(UN):
                s = b * SB + q * UN + i
                whole = retm[s].astype(F32)
                for j in range(4):
                    half, base = j // 2, 64 * (j % 2)
                    count = own_s[s, 16 + j]
                    keep = (lanes >= base) & (lanes < base + count)
                    value = jnp.where(keep, whole[:, half * FZ : (half + 1) * FZ], 0.0)
                    shift = (own_s[s, 8 + j] - base) & (FZ - 1)
                    tiles[j * N + s] = pltpu.roll(value, shift, 1)

    for r in range(0, DR, 2):
        pair = []
        for k in range(2):
            rows = tiles2(tiles, r + k)
            pair.append(jnp.concatenate([rows * here, rows * after], axis=0))
        got = dot_nn(group_hot, jnp.concatenate(pair, axis=1))
        cellv[r * GROUPS : (r + 1) * GROUPS] = got[:, 0:FZ]
        cellv[(r + 1) * GROUPS : (r + 2) * GROUPS] = got[:, FZ : 2 * FZ]
    for h in range(0, GROUPS // 2, 2):
        both = []
        for k in range(2):
            first = 2 * (h + k)
            both.append(
                jnp.concatenate(
                    [
                        cellv[pl.ds(first, 8, stride=GROUPS), :],
                        cellv[pl.ds(first + 1, 8, stride=GROUPS), :],
                    ],
                    axis=1,
                )
            )
        rbuf[h * 8 : (h + 2) * 8] = jnp.concatenate(both, axis=0).astype(BF16)

    @pl.loop(0, CHUNKS)
    def _(c):
        for i in range(PER):
            g = c * PER + i
            row = jnp.concatenate([cell[pl.ds(2 * g, 1), :], cell[pl.ds(2 * g + 1, 1), :]], axis=1)
            high = jnp.broadcast_to(row >> 8, (8, W))
            full = dot_nn(rbuf[...], lall[c, :, i * W : (i + 1) * W])
            got = jnp.zeros((8, W), F32)
            for h in range(GROUPS // 2):
                got = jnp.where(high == h, full[h * 8 : (h + 1) * 8], got)
            force_o[:, pl.ds(pl.multiple_of(g * W, W), W)] = live[pl.ds(g, 1), :] * (
                got - slip * keep8[g]
            )

    for copy in mig + halo:
        copy.wait_send()
    for b in range(NSB):
        wait_bytes(sendm.at[span(b)], am_ss.at[b])
        wait_bytes(sendr.at[span(b)], back_ss.at[b])


def per_device(
    particles, migrant_index, migrant_count, migrated_slot_cell, source_tile_size,
    tile_owner, tile_offset, closure, damping,
):
    vmem = pl.BlockSpec(memory_space=pltpu.VMEM)
    smem = pl.BlockSpec(memory_space=pltpu.SMEM)
    dma = pltpu.SemaphoreType.DMA
    scratch = [
        pltpu.VMEM((RES * CH, W), BF16),
        pltpu.VMEM((4, 2 * CH, MIG), BF16),
        pltpu.VMEM((4, 2 * CH, MIG), BF16),
        pltpu.VMEM((BLOCKS, W), F32),
        pltpu.VMEM((BLOCKS, 16, W), BF16),
        pltpu.VMEM((BLOCKS, 16, W), BF16),
        pltpu.VMEM((CHUNKS, W, KC), BF16),
        pltpu.VMEM((BLOCKS, 16, W), BF16),
        pltpu.VMEM((BLOCKS, 16, W), BF16),
        pltpu.VMEM((GROUPS // 2 * 9, KC), BF16),
        pltpu.VMEM((2, GROUPS // 2 * 9, FZ), F32),
        pltpu.VMEM((N, 8, W + EXT), BF16),
        pltpu.VMEM((N * 8, EXT), F32),
        pltpu.VMEM((N, 8, W + EXT), BF16),
        pltpu.VMEM((N, 128), I32),
        pltpu.SMEM((N, 128), I32),
        pltpu.VMEM((4 * N, 8, FZ), F32),
        pltpu.VMEM((4 * N, FZ), F32),
        pltpu.VMEM((DR * FX * FY, FZ), F32),
        pltpu.VMEM((DR * 4 * N, FZ), F32),
        pltpu.VMEM((DR * GROUPS, FZ), F32),
        pltpu.VMEM((N, 128), I32),
        pltpu.SMEM((N, 128), I32),
        pltpu.VMEM((BLOCKS, 8, W), F32),
        pltpu.VMEM((FX + 2, FY + 2, 8, FZ), F32),
        pltpu.VMEM((FX + 2, FY + 2, 1, FZ), F32),
        pltpu.VMEM((FX, FY * 8, FZ), F32),
        pltpu.VMEM((N, 8, W), BF16),
        pltpu.VMEM((N, 8, W), BF16),
        pltpu.VMEM((GROUPS * 4, W), BF16),
        dma((4,)), dma((4,)), dma((NSB,)), dma((NSB,)),
        dma((16,)), dma((16,)), dma((NSB,)), dma((NSB,)), dma((NSB,)), pltpu.SemaphoreType.REGULAR, dma(()),
    ]
    return pl.pallas_call(
        body,
        out_shape=(
            jax.ShapeDtypeStruct((DR, FX, FY, FZ), BF16),
            jax.ShapeDtypeStruct((DR, SLOTS), F32),
        ),
        in_specs=[vmem, vmem, smem, vmem, vmem, vmem, vmem, vmem, smem],
        out_specs=(vmem, vmem),
        scratch_shapes=scratch,
        compiler_params=pltpu.CompilerParams(
            collective_id=0, has_side_effects=True, vmem_limit_bytes=60 * 1024 * 1024
        ),
    )(
        particles,
        migrant_index,
        migrant_count,
        migrated_slot_cell.reshape(2 * BLOCKS, 128),
        source_tile_size,
        tile_owner.reshape(1, TILES),
        tile_offset.reshape(1, TILES),
        closure,
        damping,
    )


def solution(mesh):
    in_specs = (
        P(None, ("gx", "gy")),
        P(("gx", "gy"), None),
        P(("gx", "gy"), None),
        P(("gx", "gy")),
        P(("gx", "gy"), None),
        P(("gx", "gy"), None),
        P(("gx", "gy")),
        P(),
        P(),
    )
    out_specs = (P(None, "gx", "gy", None), P(None, ("gx", "gy")))
    return jax.shard_map(
        per_device, mesh=mesh, in_specs=in_specs, out_specs=out_specs, check_vma=False
    )
```
